512 devices in a mesh: pair: 32 (over y, x), row: 16 (over z, core).
Axes of the slice: x: 4, y: 8, z: 8, core: 2. Of those that a mesh axis runs over, the one named last changes fastest.
Arguments:
- r_factor: float32 [16384, 16384], P(('row', 'pair')), may hold values from -40 to 40, as said below
- block_slots: int32 [256], replicated, may hold values from 0 to 255, as said below
Outputs:
- rotated: float32 [16384, 16384], P('row', 'pair')
- off_ratio: float32 [], replicated
The draws below stay inside these ranges and needn't reach their ends.
Inputs may be any that keep to these rules, and one draw needn't show every extreme that they name: `block_slots`: each of the 256 column blocks appears exactly once. `r_factor`: entries below the diagonal are zero and the diagonal is positive.
All inputs are finite; a program needn't handle non-finite values.
Results may differ from the reference program's by a relative error of at most 0.0001.
Values sent between devices are 32-bit elements; how exact they have to be, the bound alone decides.
A program may use at most 64 MiB of HBM per device.

```python
import jax
import jax.numpy as jnp
from jax import lax

BLOCK = 64
ITERS = 3
BLOCKS = 256
ORDER = 16384


def slot_order(key):
    return jax.random.permutation(jax.random.fold_in(key, 11), BLOCKS).astype(jnp.int32)


def draw_block_slots(key, part):
    return slot_order(key)


def draw_r_factor(key, part):
    slots = slot_order(key)
    inverse = jnp.zeros((BLOCKS,), jnp.int32).at[slots].set(jnp.arange(BLOCKS, dtype=jnp.int32))
    columns = jnp.arange(ORDER, dtype=jnp.int32)
    col_block = columns // BLOCK
    col_slot = inverse[col_block]
    partner_block = slots[jnp.bitwise_xor(col_slot, 1)]
    partner_col = partner_block * BLOCK + columns % BLOCK
    level = 0.3 * 10.0 ** (col_slot.astype(jnp.float32) / (BLOCKS - 1))
    first, second, third = jax.random.split(jax.random.fold_in(key, 5), 3)
    noise = jnp.clip(jax.random.normal(first, (ORDER, ORDER), jnp.float32), -4.0, 4.0)
    factor = jnp.exp(jax.random.uniform(second, (ORDER,), jnp.float32, 0.0, 0.9))
    mixed = noise + 0.35 * noise[:, partner_col] + 0.5 * jnp.roll(noise, 1, axis=1)
    row_ids = jnp.arange(ORDER, dtype=jnp.int32)[:, None]
    upper = row_ids < columns[None, :]
    spread = mixed / jnp.sqrt(columns.astype(jnp.float32) + 1.0)[None, :]
    diag_vals = 1.0 + 0.5 * jax.random.uniform(third, (ORDER,), jnp.float32)
    entries = jnp.where(upper, spread, 0.0) + jnp.where(row_ids == columns[None, :], diag_vals[None, :], 0.0)
    return (entries * (level * factor)[None, :]).astype(jnp.float32)


def setup_inputs(seed: int = 0) -> dict:
    key_of = jax.random.split(jax.random.key(seed), 3)
    return {
        "r_factor": draw_r_factor(jax.random.fold_in(key_of[2], 71), 0),
        "block_slots": draw_block_slots(jax.random.fold_in(key_of[2], 71), 0),
    }


def cayley(pair_gram):
    size_n = pair_gram.shape[0]
    diag_vals = jnp.diagonal(pair_gram)
    spread = diag_vals[:, None] - diag_vals[None, :]
    denom = 2.0 * (diag_vals[:, None] ** 2 + diag_vals[None, :] ** 2)
    skew_part = pair_gram * spread / denom
    unit_matrix = jnp.eye(size_n, dtype=pair_gram.dtype)
    minus_part = unit_matrix - skew_part
    system = unit_matrix - jnp.dot(skew_part, skew_part, precision=lax.Precision.HIGHEST)
    product = jnp.dot(minus_part, minus_part, precision=lax.Precision.HIGHEST)
    factor = jnp.linalg.cholesky(system)
    return jax.scipy.linalg.cho_solve((factor, True), product.T).T

def reference(r_factor, block_slots):
    pair_width = 2 * BLOCK
    pair_total = BLOCKS // 2
    unit_mask = jnp.eye(pair_width, dtype=jnp.bool_)

    def solve_pair(pair_index, carry):
        rotated, off_total, diag_total = carry
        first_block = block_slots[2 * pair_index].astype(jnp.int32)
        second_block = block_slots[2 * pair_index + 1].astype(jnp.int32)
        column = jnp.concatenate([lax.dynamic_slice_in_dim(r_factor, (first_block * BLOCK).astype(jnp.int32), BLOCK, 1), lax.dynamic_slice_in_dim(r_factor, (second_block * BLOCK).astype(jnp.int32), BLOCK, 1)], axis=1)
        for sweep in range(ITERS):
            pair_gram = jnp.dot(column.T, column, precision=lax.Precision.HIGHEST)
            if sweep == 0:
                squares = pair_gram * pair_gram
                off_total = off_total + jnp.sum(jnp.where(unit_mask, 0.0, squares))
                diag_total = diag_total + jnp.sum(jnp.where(unit_mask, squares, 0.0))
            column = jnp.dot(column, cayley(pair_gram), precision=lax.Precision.HIGHEST)
        upper_slot = jnp.where(pair_index == 0, 0, jnp.where(pair_index == pair_total - 1, 2 * pair_index + 1, 2 * pair_index + 2)).astype(jnp.int32)
        lower_slot = jnp.where(pair_index == 0, 2, 2 * pair_index - 1).astype(jnp.int32)
        zero_index = jnp.zeros((), jnp.int32)
        rotated = lax.dynamic_update_slice(rotated, column[:, :BLOCK], (zero_index, (upper_slot * BLOCK).astype(jnp.int32)))
        rotated = lax.dynamic_update_slice(rotated, column[:, BLOCK:], (zero_index, (lower_slot * BLOCK).astype(jnp.int32)))
        return (rotated, off_total, diag_total)
    start = (jnp.zeros_like(r_factor), jnp.zeros((), r_factor.dtype), jnp.zeros((), r_factor.dtype))
    rotated, off_total, diag_total = lax.fori_loop(0, pair_total, solve_pair, start)
    off_ratio = jnp.sqrt(off_total / diag_total)
    return (rotated, off_ratio)
```

```python
import functools

import jax
import jax.numpy as jnp
from jax import lax
from jax.experimental import pallas as pl
from jax.experimental.pallas import tpu as pltpu
from jax.sharding import PartitionSpec as P

BLOCK = 64
ITERS = 3
WIDTH = 2 * BLOCK
MESH = pl.DeviceIdType.MESH
HIGHEST = lax.Precision.HIGHEST
NEUMANN_TOL = 1e-8
X_CHIPS = 4


def mm(lhs, rhs, lhs_dim=1):
    return lax.dot_general(
        lhs,
        rhs,
        (((lhs_dim,), (0,)), ((), ())),
        precision=HIGHEST,
        preferred_element_type=jnp.float32,
    )


def lanes(shape):
    return lax.broadcasted_iota(jnp.int32, shape, len(shape) - 1)


def arrange_kernel(slots_ref, r_ref, out_ref):
    group = pl.program_id(0)
    rows = r_ref.shape[0]
    low = lanes((rows, WIDTH)) < BLOCK
    for pair in range(out_ref.shape[2] // WIDTH):
        halves = []
        for side in range(2):
            block = slots_ref[group * (out_ref.shape[2] // BLOCK) + 2 * pair + side]
            tile = r_ref[:, pl.ds(pl.multiple_of((block // 2) * WIDTH, WIDTH), WIDTH)]
            halves.append(pltpu.roll(tile, ((block + side) % 2) * BLOCK, 1))
        out_ref[0, :, pair * WIDTH : (pair + 1) * WIDTH] = jnp.where(low, halves[0], halves[1])


def arrange(r_factor, block_slots, groups):
    rows, cols = r_factor.shape
    return pl.pallas_call(
        arrange_kernel,
        out_shape=jax.ShapeDtypeStruct((groups, rows, cols // groups), jnp.float32),
        grid_spec=pltpu.PrefetchScalarGridSpec(
            num_scalar_prefetch=1,
            grid=(groups,),
            in_specs=[pl.BlockSpec((rows, cols), lambda g, s: (0, 0))],
            out_specs=pl.BlockSpec((1, rows, cols // groups), lambda g, s: (g, 0, 0)),
        ),
    )(block_slots, r_factor)


def gram_kernel(
    zs, x_ref, out_ref, part, half_in, mine, z_in, full,
    half_send, half_recv, rs_send, rs_recv, ag_send, ag_recv,
):
    row = lax.axis_index("row")
    z, core = row // 2, row % 2
    other = z * 2 + (1 - core)
    half = mine.shape[0]
    chunk = half // zs

    def peer(k):
        return lax.rem(z + k, zs)

    barrier = pltpu.get_barrier_semaphore()
    pl.semaphore_signal(barrier, inc=1, device_id={"row": other}, device_id_type=MESH)
    for k in range(1, zs):
        pl.semaphore_signal(
            barrier, inc=1, device_id={"row": peer(k) * 2 + core}, device_id_type=MESH
        )

    def gram(side):
        for i in range(half // WIDTH):
            at = pl.multiple_of(side * half + i * WIDTH, WIDTH)
            cols = x_ref[:, pl.ds(at, WIDTH)]
            part[pl.ds(at, WIDTH), :] = mm(cols, cols, 0)

    gram(1 - core)
    pl.semaphore_wait(barrier, zs)
    swap = pltpu.make_async_remote_copy(
        src_ref=part.at[pl.ds(pl.multiple_of((1 - core) * half, half), half)],
        dst_ref=half_in,
        send_sem=half_send,
        recv_sem=half_recv,
        device_id={"row": other},
        device_id_type=MESH,
    )
    swap.start()
    gram(core)
    swap.wait()
    mine[...] = part[pl.ds(pl.multiple_of(core * half, half), half), :] + half_in[...]

    def scatter(k):
        return pltpu.make_async_remote_copy(
            src_ref=mine.at[pl.ds(pl.multiple_of(peer(k) * chunk, chunk), chunk)],
            dst_ref=z_in.at[zs - k],
            send_sem=rs_send.at[k],
            recv_sem=rs_recv.at[zs - k],
            device_id={"row": peer(k) * 2 + core},
            device_id_type=MESH,
        )

    for k in range(1, zs):
        scatter(k).start()
    own = pl.ds(pl.multiple_of(z * chunk, chunk), chunk)
    for k in range(1, zs):
        scatter(k).wait()
    total = mine[own, :]
    for k in range(1, zs):
        total = total + z_in[k]
    full[own, :] = total

    def gather(k):
        return pltpu.make_async_remote_copy(
            src_ref=full.at[own],
            dst_ref=full.at[own],
            send_sem=ag_send.at[k],
            recv_sem=ag_recv.at[zs - k],
            device_id={"row": peer(k) * 2 + core},
            device_id_type=MESH,
        )

    for k in range(1, zs):
        gather(k).start()
    for k in range(1, zs):
        gather(k).wait()
    out_ref[...] = full[...]


def half_grams(column):
    rows, cols = column.shape
    half = cols // 2
    zs = lax.axis_size("row") // 2
    vmem = pl.BlockSpec(memory_space=pltpu.VMEM)
    dma = pltpu.SemaphoreType.DMA
    return pl.pallas_call(
        functools.partial(gram_kernel, zs),
        out_shape=jax.ShapeDtypeStruct((half, WIDTH), jnp.float32),
        in_specs=[vmem],
        out_specs=vmem,
        scratch_shapes=[
            pltpu.VMEM((cols, WIDTH), jnp.float32),
            pltpu.VMEM((half, WIDTH), jnp.float32),
            pltpu.VMEM((half, WIDTH), jnp.float32),
            pltpu.VMEM((zs, half // zs, WIDTH), jnp.float32),
            pltpu.VMEM((half, WIDTH), jnp.float32),
            dma,
            dma,
            dma((zs,)),
            dma((zs,)),
            dma((zs,)),
            dma((zs,)),
        ],
        compiler_params=pltpu.CompilerParams(collective_id=0, has_side_effects=True),
    )(column)


def rotation_kernel(g_ref, out_ref, gram, basis, power, turn):
    pairs = gram.shape[0]
    row_ids = lax.broadcasted_iota(jnp.int32, (WIDTH, WIDTH), 0)
    unit = row_ids == lanes((WIDTH, WIDTH))
    eye = jnp.where(unit, 1.0, 0.0).astype(jnp.float32)
    off = jnp.zeros((1, WIDTH), jnp.float32)
    on = jnp.zeros((1, WIDTH), jnp.float32)
    for p in range(pairs):
        value = g_ref[p * WIDTH : (p + 1) * WIDTH, :]
        gram[p] = value
        squares = value * value
        off = off + jnp.sum(jnp.where(unit, 0.0, squares), axis=0, keepdims=True)
        on = on + jnp.sum(jnp.where(unit, squares, 0.0), axis=0, keepdims=True)
    tile_row = lax.broadcasted_iota(jnp.int32, (8, WIDTH), 0)
    out_ref[pairs * WIDTH : pairs * WIDTH + 8, :] = jnp.where(
        tile_row == 0, off, jnp.where(tile_row == 1, on, 0.0)
    )

    for sweep in range(ITERS):
        ratio = jnp.zeros((), jnp.float32)
        for p in range(pairs):
            value = gram[p]
            on_diag = jnp.where(unit, value, 0.0)
            d_col = jnp.sum(on_diag, axis=1, keepdims=True)
            d_row = jnp.sum(on_diag, axis=0, keepdims=True)
            skew = value * (d_col - d_row) / (2.0 * (d_col * d_col + d_row * d_row))
            square = mm(skew, skew)
            bound = jnp.max(jnp.sum(jnp.abs(square), axis=0, keepdims=True))
            scale = 2.0 / (2.0 + bound)
            power[p] = eye - scale * (eye - square)
            turn[p] = scale * (eye - 2.0 * skew + square)
            ratio = jnp.maximum(ratio, bound / (2.0 + bound))

        def step(carry):
            for p in range(pairs):
                e = power[p]
                v = turn[p]
                turn[p] = v + mm(v, e)
                power[p] = mm(e, e)
            return carry * carry

        lax.while_loop(lambda left: left > NEUMANN_TOL, step, ratio)
        for p in range(pairs):
            v = turn[p]
            if sweep + 1 < ITERS:
                gram[p] = mm(v, mm(gram[p], v), 0)
            if sweep == 0:
                basis[p] = v
            elif sweep + 1 < ITERS:
                basis[p] = mm(basis[p], v)
            else:
                out_ref[p * WIDTH : (p + 1) * WIDTH, :] = mm(basis[p], v)


def rotations(grams):
    vmem = pl.BlockSpec(memory_space=pltpu.VMEM)
    pairs = grams.shape[0] // WIDTH
    work = pltpu.VMEM((pairs, WIDTH, WIDTH), jnp.float32)
    return pl.pallas_call(
        rotation_kernel,
        out_shape=jax.ShapeDtypeStruct((grams.shape[0] + 8, WIDTH), jnp.float32),
        in_specs=[vmem],
        out_specs=vmem,
        scratch_shapes=[work] * 4,
    )(grams)


def apply_kernel(
    xs, ys, x_ref, v_ref, out_ref, ratio_ref,
    v_in, turned, packed, landed, sum_x, sum_y,
    v_send, v_recv, edge_send, edge_recv, x_send, x_recv, y_send, y_recv,
):
    pair = lax.axis_index("pair")
    row = lax.axis_index("row")
    core = row % 2
    other = (row // 2) * 2 + (1 - core)
    count = xs * ys
    y, x = pair // xs, pair % xs
    rows = x_ref.shape[0]
    half = rows // 2
    vrows = v_ref.shape[0] - 8

    def x_peer(k):
        return y * xs + lax.rem(x + k, xs)

    def y_peer(k):
        return lax.rem(y + k, ys) * xs + x

    right, left = lax.rem(pair + 1, count), lax.rem(pair + count - 1, count)
    barrier = pltpu.get_barrier_semaphore()
    pl.semaphore_signal(barrier, inc=1, device_id={"row": other}, device_id_type=MESH)
    peers = [left, right] + [x_peer(k) for k in range(1, xs)] + [y_peer(k) for k in range(1, ys)]
    for peer in peers:
        pl.semaphore_signal(barrier, inc=1, device_id={"pair": peer}, device_id_type=MESH)

    def turn(source, j, local):
        v = source[pl.ds(pl.multiple_of(local * WIDTH, WIDTH), WIDTH), :]
        turned[j] = mm(x_ref[:, pl.ds(pl.multiple_of(j * WIDTH, WIDTH), WIDTH)], v)

    lane = lanes((half, WIDTH))

    def edge(side):
        value = turned.at[3 * side]
        keep = (lane < BLOCK) == (side == 1)
        packed[side] = jnp.where(keep, value[0:half, :], pltpu.roll(value[half:rows, :], BLOCK, 1))

    def edge_copy(side):
        return pltpu.make_async_remote_copy(
            src_ref=packed.at[side],
            dst_ref=landed.at[side],
            send_sem=edge_send.at[side],
            recv_sem=edge_recv.at[side],
            device_id={"pair": lax.rem(pair + count + 2 * side - 1, count)},
            device_id_type=MESH,
        )

    away = 1 - core
    turn(v_ref, 3 * core, core)
    edge(core)
    pl.semaphore_wait(barrier, len(peers) + 1)
    swap = pltpu.make_async_remote_copy(
        src_ref=v_ref,
        dst_ref=v_in,
        send_sem=v_send,
        recv_sem=v_recv,
        device_id={"row": other},
        device_id_type=MESH,
    )
    swap.start()
    edge_copy(core).start()
    turn(v_ref, 1 + core, away)
    swap.wait()
    turn(v_in, 3 * away, away)
    edge(away)
    edge_copy(away).start()

    sum_x[x] = v_ref[vrows : vrows + 8, :] + v_in[vrows : vrows + 8, :]

    def x_copy(k):
        return pltpu.make_async_remote_copy(
            src_ref=sum_x.at[x],
            dst_ref=sum_x.at[x],
            send_sem=x_send.at[k],
            recv_sem=x_recv.at[xs - k],
            device_id={"pair": x_peer(k)},
            device_id_type=MESH,
        )

    for k in range(1, xs):
        x_copy(k).start()
    turn(v_in, 2 - core, core)
    for k in range(1, xs):
        x_copy(k).wait()
    total = sum_x[0]
    for k in range(1, xs):
        total = total + sum_x[k]
    sum_y[y] = total

    def y_copy(k):
        return pltpu.make_async_remote_copy(
            src_ref=sum_y.at[y],
            dst_ref=sum_y.at[y],
            send_sem=y_send.at[k],
            recv_sem=y_recv.at[ys - k],
            device_id={"pair": y_peer(k)},
            device_id_type=MESH,
        )

    for k in range(1, ys):
        y_copy(k).start()

    low = lanes((rows, WIDTH)) < BLOCK
    first, last = pair == 0, pair == count - 1
    out_ref[:, 2 * WIDTH : 3 * WIDTH] = jnp.where(low, turned[1], turned[3])
    upper = jnp.where(first, pltpu.roll(turned[0], BLOCK, 1), turned[0])
    out_ref[:, WIDTH : 2 * WIDTH] = jnp.where(low, upper, turned[2])

    for k in range(1, ys):
        y_copy(k).wait()
    total = sum_y[0]
    for k in range(1, ys):
        total = total + sum_y[k]
    off = jnp.sum(total[0:1, :], axis=1, keepdims=True)
    on = jnp.sum(total[1:2, :], axis=1, keepdims=True)
    ratio_ref[...] = jnp.broadcast_to(jnp.sqrt(off / on), ratio_ref.shape)

    edge_copy(core).wait()
    edge_copy(away).wait()
    down = jnp.concatenate([landed[0], pltpu.roll(landed[0], BLOCK, 1)], axis=0)
    down = jnp.where(last, pltpu.roll(turned[3], BLOCK, 1), down)
    out_ref[:, 3 * WIDTH : 4 * WIDTH] = jnp.where(low, turned[2], down)
    up = jnp.concatenate([landed[1], pltpu.roll(landed[1], BLOCK, 1)], axis=0)
    up = jnp.where(first, turned[0], up)
    out_ref[:, 0:WIDTH] = jnp.where(low, up, turned[1])


def apply_and_move(column, turns):
    rows, cols = column.shape
    count = lax.axis_size("pair")
    xs = X_CHIPS
    ys = count // xs
    vmem = pl.BlockSpec(memory_space=pltpu.VMEM)
    dma = pltpu.SemaphoreType.DMA
    return pl.pallas_call(
        functools.partial(apply_kernel, xs, ys),
        out_shape=(
            jax.ShapeDtypeStruct((rows, cols), jnp.float32),
            jax.ShapeDtypeStruct((8, WIDTH), jnp.float32),
        ),
        in_specs=[vmem, vmem],
        out_specs=(vmem, vmem),
        scratch_shapes=[
            pltpu.VMEM(turns.shape, jnp.float32),
            pltpu.VMEM((cols // WIDTH, rows, WIDTH), jnp.float32),
            pltpu.VMEM((2, rows // 2, WIDTH), jnp.float32),
            pltpu.VMEM((2, rows // 2, WIDTH), jnp.float32),
            pltpu.VMEM((xs, 8, WIDTH), jnp.float32),
            pltpu.VMEM((ys, 8, WIDTH), jnp.float32),
            dma,
            dma,
            dma((2,)),
            dma((2,)),
            dma((xs,)),
            dma((xs,)),
            dma((ys,)),
            dma((ys,)),
        ],
        compiler_params=pltpu.CompilerParams(collective_id=1, has_side_effects=True),
    )(column, turns)


def on_device(r_factor, block_slots):
    rows_in, total_cols = r_factor.shape
    count = lax.axis_size("pair")
    slabs = arrange(r_factor, block_slots, count)
    received = lax.all_to_all(slabs, "pair", split_axis=0, concat_axis=0, tiled=True)
    column = received.reshape(rows_in * count, total_cols // count)
    turns = rotations(half_grams(column))
    rotated, ratio = apply_and_move(column, turns)
    return (rotated, ratio[0, 0])


def solution(mesh):
    in_specs = (P(("row", "pair"), None), P())
    out_specs = (P("row", "pair"), P())
    return jax.shard_map(
        on_device, mesh=mesh, in_specs=in_specs, out_specs=out_specs, check_vma=False
    )
```

```python
import functools

import jax
import jax.numpy as jnp
from jax import lax
from jax.experimental import pallas as pl
from jax.experimental.pallas import tpu as pltpu
from jax.sharding import PartitionSpec as P

BLOCK = 64
ITERS = 3
WIDTH = 2 * BLOCK
MESH = pl.DeviceIdType.MESH
HIGHEST = lax.Precision.HIGHEST
NEUMANN_TOL = 1e-8
X_CHIPS = 4
EARLY = 8


def mm(lhs, rhs, lhs_dim=1):
    return lax.dot_general(
        lhs,
        rhs,
        (((lhs_dim,), (0,)), ((), ())),
        precision=HIGHEST,
        preferred_element_type=jnp.float32,
    )


def lanes(shape):
    return lax.broadcasted_iota(jnp.int32, shape, len(shape) - 1)


def spread_kernel(
    count, zs, slots_ref, r_ref, x_ref, g_ref,
    blocks, stage, held, part, half_in, mine, z_in, full,
    out_send, out_recv, half_send, half_recv, rs_send, rs_recv, ag_send, ag_recv, save_sem,
):
    me = lax.axis_index("pair")
    row = lax.axis_index("row")
    z, core = row // 2, row % 2
    other = z * 2 + (1 - core)
    rows = r_ref.shape[0]
    steps = held.shape[0]
    half = mine.shape[1]
    chunk = half // zs
    low = lanes((rows, WIDTH)) < BLOCK

    def target(k):
        return lax.rem(me + k, count)

    def z_row(k):
        return lax.rem(z + k, zs) * 2 + core

    barrier = pltpu.get_barrier_semaphore()
    pl.semaphore_signal(barrier, inc=1, device_id={"row": other}, device_id_type=MESH)
    for k in range(1, zs):
        pl.semaphore_signal(barrier, inc=1, device_id={"row": z_row(k)}, device_id_type=MESH)

    def greet(k, carry):
        pl.semaphore_signal(barrier, inc=1, device_id={"pair": target(k)}, device_id_type=MESH)
        return carry

    lax.fori_loop(1, count, greet, 0)

    def lift(t, carry):
        tile = r_ref[:, pl.ds(pl.multiple_of(t * WIDTH, WIDTH), WIDTH)]
        blocks[2 * t] = tile
        blocks[2 * t + 1] = pltpu.roll(tile, BLOCK, 1)
        return carry

    lax.fori_loop(0, blocks.shape[0] // 2, lift, 0, unroll=8)

    def piece(group, s, i):
        slot = group * 8 + 2 * (2 * i + s)
        upper = blocks[slots_ref[slot]]
        lower = blocks[slots_ref[slot + 1]]
        return jnp.where(low, upper, pltpu.roll(lower, BLOCK, 1))

    def arrange(s):
        def body(k, carry):
            group = target(k)
            for i in range(2):
                stage[s, group, :, i * WIDTH : (i + 1) * WIDTH] = piece(group, s, i)
            return carry

        return body

    here = pl.ds(pl.multiple_of(me * rows, rows), rows)

    def send(s, k):
        return pltpu.make_async_remote_copy(
            src_ref=stage.at[s, target(k)],
            dst_ref=held.at[s, here],
            send_sem=out_send.at[s, k],
            recv_sem=out_recv.at[s, count - k],
            device_id={"pair": target(k)},
            device_id_type=MESH,
        )

    def start(s):
        def body(k, carry):
            send(s, k).start()
            return carry

        return body

    def both(s):
        def body(k, carry):
            arrange(s)(k, carry)
            send(s, k).start()
            return carry

        return body

    def finish(s):
        def body(k, carry):
            send(s, k).wait()
            return carry

        return body

    lax.fori_loop(1, EARLY, arrange(0), 0)
    pl.semaphore_wait(barrier, count + zs - 1)
    lax.fori_loop(1, EARLY, start(0), 0)
    lax.fori_loop(EARLY, count, both(0), 0)
    for s in range(1, steps):
        lax.fori_loop(1, count, both(s), 0)
    for s in range(steps):
        for i in range(2):
            held[s, here, i * WIDTH : (i + 1) * WIDTH] = piece(me, s, i)

    def gram(s, i):
        cols = held[s, :, pl.ds(pl.multiple_of(i * WIDTH, WIDTH), WIDTH)]
        part[s, pl.ds(pl.multiple_of(i * WIDTH, WIDTH), WIDTH), :] = mm(cols, cols, 0)

    own = pl.ds(pl.multiple_of(z * chunk, chunk), chunk)
    for s in range(steps):
        lax.fori_loop(1, count, finish(s), 0)
        save = pltpu.make_async_copy(held.at[s], x_ref.at[s], save_sem.at[s])
        save.start()
        gram(s, 1 - core)
        swap = pltpu.make_async_remote_copy(
            src_ref=part.at[s, pl.ds(pl.multiple_of((1 - core) * half, half), half)],
            dst_ref=half_in.at[s],
            send_sem=half_send.at[s],
            recv_sem=half_recv.at[s],
            device_id={"row": other},
            device_id_type=MESH,
        )
        swap.start()
        gram(s, core)
        swap.wait()
        mine[s] = part[s, pl.ds(pl.multiple_of(core * half, half), half), :] + half_in[s]

        def scatter(k, s=s):
            at = pl.multiple_of(lax.rem(z + k, zs) * chunk, chunk)
            return pltpu.make_async_remote_copy(
                src_ref=mine.at[s, pl.ds(at, chunk)],
                dst_ref=z_in.at[s, zs - k],
                send_sem=rs_send.at[s, k],
                recv_sem=rs_recv.at[s, zs - k],
                device_id={"row": z_row(k)},
                device_id_type=MESH,
            )

        for k in range(1, zs):
            scatter(k).start()
        for k in range(1, zs):
            scatter(k).wait()
        total = mine[s, own, :]
        for k in range(1, zs):
            total = total + z_in[s, k]
        full[s, own, :] = total

        def gather(k, s=s):
            return pltpu.make_async_remote_copy(
                src_ref=full.at[s, own],
                dst_ref=full.at[s, own],
                send_sem=ag_send.at[s, k],
                recv_sem=ag_recv.at[s, zs - k],
                device_id={"row": z_row(k)},
                device_id_type=MESH,
            )

        for k in range(1, zs):
            gather(k).start()
        for k in range(1, zs):
            gather(k).wait()
        g_ref[s * half : (s + 1) * half, :] = full[s]
        save.wait()


def spread(r_factor, block_slots):
    rows, cols = r_factor.shape
    count = lax.axis_size("pair")
    zs = lax.axis_size("row") // 2
    steps = 2
    wide = cols // count // steps
    half = WIDTH
    vmem = pl.BlockSpec(memory_space=pltpu.VMEM)
    dma = pltpu.SemaphoreType.DMA
    return pl.pallas_call(
        functools.partial(spread_kernel, count, zs),
        out_shape=(
            jax.ShapeDtypeStruct((steps, rows * count, wide), jnp.float32),
            jax.ShapeDtypeStruct((steps * half, WIDTH), jnp.float32),
        ),
        in_specs=[pl.BlockSpec(memory_space=pltpu.SMEM), vmem],
        out_specs=(pl.BlockSpec(memory_space=pl.ANY), vmem),
        scratch_shapes=[
            pltpu.VMEM((cols // BLOCK, rows, WIDTH), jnp.float32),
            pltpu.VMEM((steps, count, rows, wide), jnp.float32),
            pltpu.VMEM((steps, rows * count, wide), jnp.float32),
            pltpu.VMEM((steps, 2 * half, WIDTH), jnp.float32),
            pltpu.VMEM((steps, half, WIDTH), jnp.float32),
            pltpu.VMEM((steps, half, WIDTH), jnp.float32),
            pltpu.VMEM((steps, zs, half // zs, WIDTH), jnp.float32),
            pltpu.VMEM((steps, half, WIDTH), jnp.float32),
            dma((steps, count)),
            dma((steps, count)),
            dma((steps,)),
            dma((steps,)),
            dma((steps, zs)),
            dma((steps, zs)),
            dma((steps, zs)),
            dma((steps, zs)),
            dma((steps,)),
        ],
        compiler_params=pltpu.CompilerParams(collective_id=0, has_side_effects=True),
    )(block_slots, r_factor)


def rotation_kernel(g_ref, out_ref, gram, basis, power, turn):
    pairs = gram.shape[0]
    row_ids = lax.broadcasted_iota(jnp.int32, (WIDTH, WIDTH), 0)
    unit = row_ids == lanes((WIDTH, WIDTH))
    eye = jnp.where(unit, 1.0, 0.0).astype(jnp.float32)
    off = jnp.zeros((1, WIDTH), jnp.float32)
    on = jnp.zeros((1, WIDTH), jnp.float32)
    for p in range(pairs):
        value = g_ref[p * WIDTH : (p + 1) * WIDTH, :]
        gram[p] = value
        squares = value * value
        off = off + jnp.sum(jnp.where(unit, 0.0, squares), axis=0, keepdims=True)
        on = on + jnp.sum(jnp.where(unit, squares, 0.0), axis=0, keepdims=True)
    tile_row = lax.broadcasted_iota(jnp.int32, (8, WIDTH), 0)
    out_ref[pairs * WIDTH : pairs * WIDTH + 8, :] = jnp.where(
        tile_row == 0, off, jnp.where(tile_row == 1, on, 0.0)
    )

    for sweep in range(ITERS):
        ratio = jnp.zeros((), jnp.float32)
        for p in range(pairs):
            value = gram[p]
            on_diag = jnp.where(unit, value, 0.0)
            d_col = jnp.sum(on_diag, axis=1, keepdims=True)
            d_row = jnp.sum(on_diag, axis=0, keepdims=True)
            skew = value * (d_col - d_row) / (2.0 * (d_col * d_col + d_row * d_row))
            square = mm(skew, skew)
            bound = jnp.max(jnp.sum(jnp.abs(square), axis=0, keepdims=True))
            scale = 2.0 / (2.0 + bound)
            power[p] = eye - scale * (eye - square)
            turn[p] = scale * (eye - 2.0 * skew + square)
            ratio = jnp.maximum(ratio, bound / (2.0 + bound))

        def step(carry):
            for p in range(pairs):
                e = power[p]
                v = turn[p]
                turn[p] = v + mm(v, e)
                power[p] = mm(e, e)
            return carry * carry

        lax.while_loop(lambda left: left > NEUMANN_TOL, step, ratio)
        for p in range(pairs):
            v = turn[p]
            if sweep + 1 < ITERS:
                gram[p] = mm(v, mm(gram[p], v), 0)
            if sweep == 0:
                basis[p] = v
            elif sweep + 1 < ITERS:
                basis[p] = mm(basis[p], v)
            else:
                out_ref[p * WIDTH : (p + 1) * WIDTH, :] = mm(basis[p], v)


def rotations(grams):
    vmem = pl.BlockSpec(memory_space=pltpu.VMEM)
    pairs = grams.shape[0] // WIDTH
    work = pltpu.VMEM((pairs, WIDTH, WIDTH), jnp.float32)
    return pl.pallas_call(
        rotation_kernel,
        out_shape=jax.ShapeDtypeStruct((grams.shape[0] + 8, WIDTH), jnp.float32),
        in_specs=[vmem],
        out_specs=vmem,
        scratch_shapes=[work] * 4,
    )(grams)


def apply_kernel(
    xs, ys, x_hbm, v_ref, out_ref, ratio_ref,
    x_ref, v_in, turned, packed, landed, sum_x, sum_y,
    x_sem, v_send, v_recv, edge_send, edge_recv, x_send, x_recv, y_send, y_recv,
):
    load = pltpu.make_async_copy(x_hbm, x_ref, x_sem)
    load.start()
    pair = lax.axis_index("pair")
    row = lax.axis_index("row")
    core = row % 2
    other = (row // 2) * 2 + (1 - core)
    count = xs * ys
    y, x = pair // xs, pair % xs
    rows = x_ref.shape[1]
    half = rows // 2
    vrows = v_ref.shape[0] - 8

    def x_peer(k):
        return y * xs + lax.rem(x + k, xs)

    def y_peer(k):
        return lax.rem(y + k, ys) * xs + x

    right, left = lax.rem(pair + 1, count), lax.rem(pair + count - 1, count)
    barrier = pltpu.get_barrier_semaphore()
    pl.semaphore_signal(barrier, inc=1, device_id={"row": other}, device_id_type=MESH)
    peers = [left, right] + [x_peer(k) for k in range(1, xs)] + [y_peer(k) for k in range(1, ys)]
    for peer in peers:
        pl.semaphore_signal(barrier, inc=1, device_id={"pair": peer}, device_id_type=MESH)

    def turn(source, j, local):
        v = source[pl.ds(pl.multiple_of(local * WIDTH, WIDTH), WIDTH), :]
        at = pl.multiple_of((j // 2) * WIDTH, WIDTH)
        turned[j] = mm(x_ref[j % 2, :, pl.ds(at, WIDTH)], v)

    lane = lanes((half, WIDTH))

    def edge(side):
        value = turned.at[3 * side]
        keep = (lane < BLOCK) == (side == 1)
        packed[side] = jnp.where(keep, value[0:half, :], pltpu.roll(value[half:rows, :], BLOCK, 1))

    def edge_copy(side):
        return pltpu.make_async_remote_copy(
            src_ref=packed.at[side],
            dst_ref=landed.at[side],
            send_sem=edge_send.at[side],
            recv_sem=edge_recv.at[side],
            device_id={"pair": lax.rem(pair + count + 2 * side - 1, count)},
            device_id_type=MESH,
        )

    away = 1 - core
    load.wait()
    turn(v_ref, 3 * core, core)
    edge(core)
    pl.semaphore_wait(barrier, len(peers) + 1)
    swap = pltpu.make_async_remote_copy(
        src_ref=v_ref,
        dst_ref=v_in,
        send_sem=v_send,
        recv_sem=v_recv,
        device_id={"row": other},
        device_id_type=MESH,
    )
    swap.start()
    edge_copy(core).start()
    turn(v_ref, 1 + core, away)
    swap.wait()
    turn(v_in, 3 * away, away)
    edge(away)
    edge_copy(away).start()

    sum_x[x] = v_ref[vrows : vrows + 8, :] + v_in[vrows : vrows + 8, :]

    def x_copy(k):
        return pltpu.make_async_remote_copy(
            src_ref=sum_x.at[x],
            dst_ref=sum_x.at[x],
            send_sem=x_send.at[k],
            recv_sem=x_recv.at[xs - k],
            device_id={"pair": x_peer(k)},
            device_id_type=MESH,
        )

    for k in range(1, xs):
        x_copy(k).start()
    turn(v_in, 2 - core, core)
    for k in range(1, xs):
        x_copy(k).wait()
    total = sum_x[0]
    for k in range(1, xs):
        total = total + sum_x[k]
    sum_y[y] = total

    def y_copy(k):
        return pltpu.make_async_remote_copy(
            src_ref=sum_y.at[y],
            dst_ref=sum_y.at[y],
            send_sem=y_send.at[k],
            recv_sem=y_recv.at[ys - k],
            device_id={"pair": y_peer(k)},
            device_id_type=MESH,
        )

    for k in range(1, ys):
        y_copy(k).start()

    low = lanes((rows, WIDTH)) < BLOCK
    first, last = pair == 0, pair == count - 1
    out_ref[:, 2 * WIDTH : 3 * WIDTH] = jnp.where(low, turned[1], turned[3])
    upper = jnp.where(first, pltpu.roll(turned[0], BLOCK, 1), turned[0])
    out_ref[:, WIDTH : 2 * WIDTH] = jnp.where(low, upper, turned[2])

    for k in range(1, ys):
        y_copy(k).wait()
    total = sum_y[0]
    for k in range(1, ys):
        total = total + sum_y[k]
    off = jnp.sum(total[0:1, :], axis=1, keepdims=True)
    on = jnp.sum(total[1:2, :], axis=1, keepdims=True)
    ratio_ref[...] = jnp.broadcast_to(jnp.sqrt(off / on), ratio_ref.shape)

    edge_copy(core).wait()
    edge_copy(away).wait()
    down = jnp.concatenate([landed[0], pltpu.roll(landed[0], BLOCK, 1)], axis=0)
    down = jnp.where(last, pltpu.roll(turned[3], BLOCK, 1), down)
    out_ref[:, 3 * WIDTH : 4 * WIDTH] = jnp.where(low, turned[2], down)
    up = jnp.concatenate([landed[1], pltpu.roll(landed[1], BLOCK, 1)], axis=0)
    up = jnp.where(first, turned[0], up)
    out_ref[:, 0:WIDTH] = jnp.where(low, up, turned[1])


def apply_and_move(column, turns):
    steps, rows, wide = column.shape
    cols = steps * wide
    count = lax.axis_size("pair")
    xs = X_CHIPS
    ys = count // xs
    vmem = pl.BlockSpec(memory_space=pltpu.VMEM)
    dma = pltpu.SemaphoreType.DMA
    return pl.pallas_call(
        functools.partial(apply_kernel, xs, ys),
        out_shape=(
            jax.ShapeDtypeStruct((rows, cols), jnp.float32),
            jax.ShapeDtypeStruct((8, WIDTH), jnp.float32),
        ),
        in_specs=[pl.BlockSpec(memory_space=pl.ANY), vmem],
        out_specs=(vmem, vmem),
        scratch_shapes=[
            pltpu.VMEM(column.shape, jnp.float32),
            pltpu.VMEM(turns.shape, jnp.float32),
            pltpu.VMEM((cols // WIDTH, rows, WIDTH), jnp.float32),
            pltpu.VMEM((2, rows // 2, WIDTH), jnp.float32),
            pltpu.VMEM((2, rows // 2, WIDTH), jnp.float32),
            pltpu.VMEM((xs, 8, WIDTH), jnp.float32),
            pltpu.VMEM((ys, 8, WIDTH), jnp.float32),
            dma,
            dma,
            dma,
            dma((2,)),
            dma((2,)),
            dma((xs,)),
            dma((xs,)),
            dma((ys,)),
            dma((ys,)),
        ],
        compiler_params=pltpu.CompilerParams(collective_id=1, has_side_effects=True),
    )(column, turns)


def on_device(r_factor, block_slots):
    column, grams = spread(r_factor, block_slots)
    rotated, ratio = apply_and_move(column, rotations(grams))
    return (rotated, ratio[0, 0])


def solution(mesh):
    in_specs = (P(("row", "pair"), None), P())
    out_specs = (P("row", "pair"), P())
    return jax.shard_map(
        on_device, mesh=mesh, in_specs=in_specs, out_specs=out_specs, check_vma=False
    )
```

```python
import functools

import jax
import jax.numpy as jnp
from jax import lax
from jax.experimental import pallas as pl
from jax.experimental.pallas import tpu as pltpu
from jax.sharding import PartitionSpec as P

BLOCK = 64
ITERS = 3
WIDTH = 2 * BLOCK
MESH = pl.DeviceIdType.MESH
HIGHEST = lax.Precision.HIGHEST
NEUMANN_TOL = 1e-8
X_CHIPS = 4
EARLY = 8
PLACE_STEPS = 4


def mm(lhs, rhs, lhs_dim=1):
    return lax.dot_general(
        lhs,
        rhs,
        (((lhs_dim,), (0,)), ((), ())),
        precision=HIGHEST,
        preferred_element_type=jnp.float32,
    )


def lanes(shape):
    return lax.broadcasted_iota(jnp.int32, shape, len(shape) - 1)


def spread_kernel(
    count, zs, slots_ref, r_hbm, x_ref, g_ref,
    r_ref, blocks, stage, held, part, half_in, mine, z_in, full,
    out_send, out_recv, half_send, half_recv, rs_send, rs_recv, ag_send, ag_recv, save_sem, load_sem,
):
    load = pltpu.make_async_copy(r_hbm, r_ref, load_sem)
    load.start()
    me = lax.axis_index("pair")
    row = lax.axis_index("row")
    z, core = row // 2, row % 2
    other = z * 2 + (1 - core)
    rows = r_ref.shape[0]
    steps = held.shape[0]
    half = mine.shape[1]
    chunk = half // zs
    low = lanes((rows, WIDTH)) < BLOCK

    def target(k):
        return lax.rem(me + k, count)

    def z_row(k):
        return lax.rem(z + k, zs) * 2 + core

    barrier = pltpu.get_barrier_semaphore()
    pl.semaphore_signal(barrier, inc=1, device_id={"row": other}, device_id_type=MESH)
    for k in range(1, zs):
        pl.semaphore_signal(barrier, inc=1, device_id={"row": z_row(k)}, device_id_type=MESH)

    def greet(k, carry):
        pl.semaphore_signal(barrier, inc=1, device_id={"pair": target(k)}, device_id_type=MESH)
        return carry

    lax.fori_loop(1, count, greet, 0)

    def lift(t, carry):
        tile = r_ref[:, pl.ds(pl.multiple_of(t * WIDTH, WIDTH), WIDTH)]
        blocks[2 * t] = tile
        blocks[2 * t + 1] = pltpu.roll(tile, BLOCK, 1)
        return carry

    load.wait()
    lax.fori_loop(0, blocks.shape[0] // 2, lift, 0, unroll=8)

    def piece(group, s, i):
        slot = group * 8 + 2 * (2 * i + s)
        upper = blocks[slots_ref[slot]]
        lower = blocks[slots_ref[slot + 1]]
        return jnp.where(low, upper, pltpu.roll(lower, BLOCK, 1))

    def arrange(s):
        def body(k, carry):
            group = target(k)
            for i in range(2):
                stage[s, group, :, i * WIDTH : (i + 1) * WIDTH] = piece(group, s, i)
            return carry

        return body

    here = pl.ds(pl.multiple_of(me * rows, rows), rows)

    def send(s, k):
        return pltpu.make_async_remote_copy(
            src_ref=stage.at[s, target(k)],
            dst_ref=held.at[s, here],
            send_sem=out_send.at[s, k],
            recv_sem=out_recv.at[s, count - k],
            device_id={"pair": target(k)},
            device_id_type=MESH,
        )

    def start(s):
        def body(k, carry):
            send(s, k).start()
            return carry

        return body

    def both(s):
        def body(k, carry):
            arrange(s)(k, carry)
            send(s, k).start()
            return carry

        return body

    def finish(s):
        def body(k, carry):
            send(s, k).wait()
            return carry

        return body

    lax.fori_loop(1, EARLY, arrange(0), 0)
    pl.semaphore_wait(barrier, count + zs - 1)
    lax.fori_loop(1, EARLY, start(0), 0)
    lax.fori_loop(EARLY, count, both(0), 0)
    for s in range(1, steps):
        lax.fori_loop(1, count, both(s), 0)
    for s in range(steps):
        for i in range(2):
            held[s, here, i * WIDTH : (i + 1) * WIDTH] = piece(me, s, i)

    def gram(s, i):
        cols = held[s, :, pl.ds(pl.multiple_of(i * WIDTH, WIDTH), WIDTH)]
        part[s, pl.ds(pl.multiple_of(i * WIDTH, WIDTH), WIDTH), :] = mm(cols, cols, 0)

    own = pl.ds(pl.multiple_of(z * chunk, chunk), chunk)
    for s in range(steps):
        lax.fori_loop(1, count, finish(s), 0)
        save = pltpu.make_async_copy(held.at[s], x_ref.at[s], save_sem.at[s])
        save.start()
        gram(s, 1 - core)
        swap = pltpu.make_async_remote_copy(
            src_ref=part.at[s, pl.ds(pl.multiple_of((1 - core) * half, half), half)],
            dst_ref=half_in.at[s],
            send_sem=half_send.at[s],
            recv_sem=half_recv.at[s],
            device_id={"row": other},
            device_id_type=MESH,
        )
        swap.start()
        gram(s, core)
        swap.wait()
        mine[s] = part[s, pl.ds(pl.multiple_of(core * half, half), half), :] + half_in[s]

        def scatter(k, s=s):
            at = pl.multiple_of(lax.rem(z + k, zs) * chunk, chunk)
            return pltpu.make_async_remote_copy(
                src_ref=mine.at[s, pl.ds(at, chunk)],
                dst_ref=z_in.at[s, zs - k],
                send_sem=rs_send.at[s, k],
                recv_sem=rs_recv.at[s, zs - k],
                device_id={"row": z_row(k)},
                device_id_type=MESH,
            )

        for k in range(1, zs):
            scatter(k).start()
        for k in range(1, zs):
            scatter(k).wait()
        total = mine[s, own, :]
        for k in range(1, zs):
            total = total + z_in[s, k]
        full[s, own, :] = total

        def gather(k, s=s):
            return pltpu.make_async_remote_copy(
                src_ref=full.at[s, own],
                dst_ref=full.at[s, own],
                send_sem=ag_send.at[s, k],
                recv_sem=ag_recv.at[s, zs - k],
                device_id={"row": z_row(k)},
                device_id_type=MESH,
            )

        for k in range(1, zs):
            gather(k).start()
        for k in range(1, zs):
            gather(k).wait()
        g_ref[s * half : (s + 1) * half, :] = full[s]
        save.wait()


def spread(r_factor, block_slots):
    rows, cols = r_factor.shape
    count = lax.axis_size("pair")
    zs = lax.axis_size("row") // 2
    steps = 2
    wide = cols // count // steps
    half = WIDTH
    vmem = pl.BlockSpec(memory_space=pltpu.VMEM)
    dma = pltpu.SemaphoreType.DMA
    return pl.pallas_call(
        functools.partial(spread_kernel, count, zs),
        out_shape=(
            jax.ShapeDtypeStruct((steps, rows * count, wide), jnp.float32),
            jax.ShapeDtypeStruct((steps * half, WIDTH), jnp.float32),
        ),
        in_specs=[pl.BlockSpec(memory_space=pltpu.SMEM), pl.BlockSpec(memory_space=pl.ANY)],
        out_specs=(pl.BlockSpec(memory_space=pl.ANY), vmem),
        scratch_shapes=[
            pltpu.VMEM((rows, cols), jnp.float32),
            pltpu.VMEM((cols // BLOCK, rows, WIDTH), jnp.float32),
            pltpu.VMEM((steps, count, rows, wide), jnp.float32),
            pltpu.VMEM((steps, rows * count, wide), jnp.float32),
            pltpu.VMEM((steps, 2 * half, WIDTH), jnp.float32),
            pltpu.VMEM((steps, half, WIDTH), jnp.float32),
            pltpu.VMEM((steps, half, WIDTH), jnp.float32),
            pltpu.VMEM((steps, zs, half // zs, WIDTH), jnp.float32),
            pltpu.VMEM((steps, half, WIDTH), jnp.float32),
            dma((steps, count)),
            dma((steps, count)),
            dma((steps,)),
            dma((steps,)),
            dma((steps, zs)),
            dma((steps, zs)),
            dma((steps, zs)),
            dma((steps, zs)),
            dma((steps,)),
            dma,
        ],
        compiler_params=pltpu.CompilerParams(collective_id=0, has_side_effects=True),
    )(block_slots, r_factor)


def rotation_kernel(g_ref, out_ref, tall, state):
    pairs = tall.shape[0]
    top, bottom = slice(0, WIDTH), slice(WIDTH, 2 * WIDTH)
    row_ids = lax.broadcasted_iota(jnp.int32, (WIDTH, WIDTH), 0)
    unit = row_ids == lanes((WIDTH, WIDTH))
    eye = jnp.where(unit, 1.0, 0.0).astype(jnp.float32)
    off = jnp.zeros((1, WIDTH), jnp.float32)
    on = jnp.zeros((1, WIDTH), jnp.float32)
    for p in range(pairs):
        value = g_ref[p * WIDTH : (p + 1) * WIDTH, :]
        tall[p, top, :] = value
        squares = value * value
        off = off + jnp.sum(jnp.where(unit, 0.0, squares), axis=0, keepdims=True)
        on = on + jnp.sum(jnp.where(unit, squares, 0.0), axis=0, keepdims=True)
    tile_row = lax.broadcasted_iota(jnp.int32, (8, WIDTH), 0)
    out_ref[pairs * WIDTH : pairs * WIDTH + 8, :] = jnp.where(
        tile_row == 0, off, jnp.where(tile_row == 1, on, 0.0)
    )

    for sweep in range(ITERS):
        ratio = jnp.zeros((), jnp.float32)
        for p in range(pairs):
            value = tall[p, top, :]
            on_diag = jnp.where(unit, value, 0.0)
            d_col = jnp.sum(on_diag, axis=1, keepdims=True)
            d_row = jnp.sum(on_diag, axis=0, keepdims=True)
            skew = value * (d_col - d_row) / (2.0 * (d_col * d_col + d_row * d_row))
            square = mm(skew, skew)
            bound = jnp.max(jnp.sum(jnp.abs(square), axis=0, keepdims=True))
            scale = 2.0 / (2.0 + bound)
            state[p, top, :] = scale * (eye - 2.0 * skew + square)
            state[p, bottom, :] = eye - scale * (eye - square)
            ratio = jnp.maximum(ratio, bound / (2.0 + bound))

        def step(carry):
            for p in range(pairs):
                both = mm(state[p], state[p, bottom, :])
                state[p, top, :] = state[p, top, :] + both[top]
                state[p, bottom, :] = both[bottom]
            return carry * carry

        lax.while_loop(lambda left: left > NEUMANN_TOL, step, ratio)
        for p in range(pairs):
            v = state[p, top, :]
            if sweep == 0:
                tall[p, top, :] = mm(v, mm(tall[p, top, :], v), 0)
                tall[p, bottom, :] = v
            elif sweep + 1 < ITERS:
                both = mm(tall[p], v)
                tall[p, top, :] = mm(v, both[top], 0)
                tall[p, bottom, :] = both[bottom]
            else:
                out_ref[p * WIDTH : (p + 1) * WIDTH, :] = mm(tall[p, bottom, :], v)


def rotations(grams):
    vmem = pl.BlockSpec(memory_space=pltpu.VMEM)
    pairs = grams.shape[0] // WIDTH
    work = pltpu.VMEM((pairs, 2 * WIDTH, WIDTH), jnp.float32)
    return pl.pallas_call(
        rotation_kernel,
        out_shape=jax.ShapeDtypeStruct((grams.shape[0] + 8, WIDTH), jnp.float32),
        in_specs=[vmem],
        out_specs=vmem,
        scratch_shapes=[work] * 2,
    )(grams)


def apply_kernel(
    xs, ys, x_hbm, v_ref, turned_hbm, landed, ratio_ref,
    x_ref, v_in, turned, packed, sum_x, sum_y,
    x_sem, save_sem, v_send, v_recv, edge_send, edge_recv, x_send, x_recv, y_send, y_recv,
):
    load = pltpu.make_async_copy(x_hbm, x_ref, x_sem)
    load.start()
    pair = lax.axis_index("pair")
    row = lax.axis_index("row")
    core = row % 2
    other = (row // 2) * 2 + (1 - core)
    count = xs * ys
    y, x = pair // xs, pair % xs
    rows = x_ref.shape[1]
    half = rows // 2
    vrows = v_in.shape[0]

    def x_peer(k):
        return y * xs + lax.rem(x + k, xs)

    def y_peer(k):
        return lax.rem(y + k, ys) * xs + x

    right, left = lax.rem(pair + 1, count), lax.rem(pair + count - 1, count)
    barrier = pltpu.get_barrier_semaphore()
    peers = [(y_peer(k), row) for k in range(1, ys)]
    peers += [(left, row), (right, row)]
    peers += [(x_peer(k), row) for k in range(1, xs)]
    peers += [(x_peer(k), other) for k in range(xs)]
    for peer in peers:
        pl.semaphore_signal(
            barrier, inc=1, device_id={"pair": peer[0], "row": peer[1]}, device_id_type=MESH
        )
    sum_x[core, x] = v_ref[vrows : vrows + 8, :]

    def turn(source, j, local):
        v = source[pl.ds(pl.multiple_of(local * WIDTH, WIDTH), WIDTH), :]
        at = pl.multiple_of((j // 2) * WIDTH, WIDTH)
        turned[j] = mm(x_ref[j % 2, :, pl.ds(at, WIDTH)], v)

    def save(j):
        return pltpu.make_async_copy(turned.at[j], turned_hbm.at[j], save_sem.at[j])

    lane = lanes((half, WIDTH))

    def edge(side):
        value = turned.at[3 * side]
        keep = (lane < BLOCK) == (side == 1)
        packed[side] = jnp.where(keep, value[0:half, :], pltpu.roll(value[half:rows, :], BLOCK, 1))

    def edge_copy(side):
        return pltpu.make_async_remote_copy(
            src_ref=packed.at[side],
            dst_ref=landed.at[side],
            send_sem=edge_send.at[side],
            recv_sem=edge_recv.at[side],
            device_id={"pair": lax.rem(pair + count + 2 * side - 1, count)},
            device_id_type=MESH,
        )

    def x_copy(k, crossed):
        return pltpu.make_async_remote_copy(
            src_ref=sum_x.at[core, x],
            dst_ref=sum_x.at[core, x],
            send_sem=x_send.at[crossed, k],
            recv_sem=x_recv.at[crossed, (xs - k) % xs],
            device_id={"pair": x_peer(k), "row": other if crossed else row},
            device_id_type=MESH,
        )

    x_copies = [x_copy(k, crossed) for crossed in range(2) for k in range(1 - crossed, xs)]

    away = 1 - core
    load.wait()
    turn(v_ref, 3 * core, core)
    edge(core)
    pl.semaphore_wait(barrier, len(peers))
    swap = pltpu.make_async_remote_copy(
        src_ref=v_ref.at[0:vrows],
        dst_ref=v_in,
        send_sem=v_send,
        recv_sem=v_recv,
        device_id={"row": other},
        device_id_type=MESH,
    )
    swap.start()
    for copy in x_copies:
        copy.start()
    edge_copy(core).start()
    save(3 * core).start()
    turn(v_ref, 1 + core, away)
    save(1 + core).start()
    swap.wait()
    turn(v_in, 3 * away, away)
    edge(away)
    edge_copy(away).start()

    for copy in x_copies:
        copy.wait()
    total = jnp.zeros((8, WIDTH), jnp.float32)
    for k in range(xs):
        total = total + (sum_x[0, k] + sum_x[1, k])
    sum_y[y] = total

    def y_copy(k):
        return pltpu.make_async_remote_copy(
            src_ref=sum_y.at[y],
            dst_ref=sum_y.at[y],
            send_sem=y_send.at[k],
            recv_sem=y_recv.at[ys - k],
            device_id={"pair": y_peer(k)},
            device_id_type=MESH,
        )

    for k in range(1, ys):
        y_copy(k).start()
    save(3 * away).start()
    turn(v_in, 2 - core, core)
    save(2 - core).start()
    for k in range(1, ys):
        y_copy(k).wait()
    total = sum_y[0]
    for k in range(1, ys):
        total = total + sum_y[k]
    off = jnp.sum(total[0:1, :], axis=1, keepdims=True)
    on = jnp.sum(total[1:2, :], axis=1, keepdims=True)
    ratio_ref[...] = jnp.broadcast_to(jnp.sqrt(off / on), ratio_ref.shape)
    for j in range(turned.shape[0]):
        save(j).wait()
    edge_copy(core).wait()
    edge_copy(away).wait()


def apply_and_move(column, turns):
    steps, rows, wide = column.shape
    pairs = steps * wide // WIDTH
    count = lax.axis_size("pair")
    xs = X_CHIPS
    ys = count // xs
    vmem = pl.BlockSpec(memory_space=pltpu.VMEM)
    hbm = pl.BlockSpec(memory_space=pl.ANY)
    dma = pltpu.SemaphoreType.DMA
    return pl.pallas_call(
        functools.partial(apply_kernel, xs, ys),
        out_shape=(
            jax.ShapeDtypeStruct((pairs, rows, WIDTH), jnp.float32),
            jax.ShapeDtypeStruct((2, rows // 2, WIDTH), jnp.float32),
            jax.ShapeDtypeStruct((8, WIDTH), jnp.float32),
        ),
        in_specs=[hbm, vmem],
        out_specs=(hbm, hbm, vmem),
        scratch_shapes=[
            pltpu.VMEM(column.shape, jnp.float32),
            pltpu.VMEM((turns.shape[0] - 8, WIDTH), jnp.float32),
            pltpu.VMEM((pairs, rows, WIDTH), jnp.float32),
            pltpu.VMEM((2, rows // 2, WIDTH), jnp.float32),
            pltpu.VMEM((2, xs, 8, WIDTH), jnp.float32),
            pltpu.VMEM((ys, 8, WIDTH), jnp.float32),
            dma,
            dma((pairs,)),
            dma,
            dma,
            dma((2,)),
            dma((2,)),
            dma((2, xs)),
            dma((2, xs)),
            dma((ys,)),
            dma((ys,)),
        ],
        compiler_params=pltpu.CompilerParams(collective_id=1, has_side_effects=True),
    )(column, turns)


def place_kernel(last_pair, turned, landed, ratio_in, out_ref, ratio_ref):
    pair = lax.axis_index("pair")
    first, last = pair == 0, pair == last_pair
    swapped = pl.program_id(0) >= pl.num_programs(0) // 2
    low = lanes(landed.shape[1:]) < BLOCK
    from_right, from_left = landed[0], landed[1]
    from_right = jnp.where(swapped, pltpu.roll(from_right, BLOCK, 1), from_right)
    from_left = jnp.where(swapped, pltpu.roll(from_left, BLOCK, 1), from_left)
    up = jnp.where(first, turned[0], from_left)
    next_up = jnp.where(first, pltpu.roll(turned[0], BLOCK, 1), turned[0])
    down = jnp.where(last, pltpu.roll(turned[3], BLOCK, 1), from_right)
    out_ref[:, 0:WIDTH] = jnp.where(low, up, turned[1])
    out_ref[:, WIDTH : 2 * WIDTH] = jnp.where(low, next_up, turned[2])
    out_ref[:, 2 * WIDTH : 3 * WIDTH] = jnp.where(low, turned[1], turned[3])
    out_ref[:, 3 * WIDTH : 4 * WIDTH] = jnp.where(low, turned[2], down)
    ratio_ref[...] = ratio_in[0:1, 0:1]


def place(turned, landed, ratio):
    pairs, rows, _ = turned.shape
    tile = rows // PLACE_STEPS
    return pl.pallas_call(
        functools.partial(place_kernel, lax.axis_size("pair") - 1),
        out_shape=(
            jax.ShapeDtypeStruct((rows, pairs * WIDTH), jnp.float32),
            jax.ShapeDtypeStruct((1, 1), jnp.float32),
        ),
        grid=(PLACE_STEPS,),
        in_specs=[
            pl.BlockSpec((pairs, tile, WIDTH), lambda g: (0, g, 0)),
            pl.BlockSpec((2, tile, WIDTH), lambda g: (0, lax.rem(g, PLACE_STEPS // 2), 0)),
            pl.BlockSpec((8, WIDTH), lambda g: (0, 0)),
        ],
        out_specs=(
            pl.BlockSpec((tile, pairs * WIDTH), lambda g: (g, 0)),
            pl.BlockSpec((1, 1), lambda g: (0, 0)),
        ),
    )(turned, landed, ratio)


def on_device(r_factor, block_slots):
    column, grams = spread(r_factor, block_slots)
    rotated, ratio = place(*apply_and_move(column, rotations(grams)))
    return (rotated, ratio.reshape(()))


def solution(mesh):
    in_specs = (P(("row", "pair"), None), P())
    out_specs = (P("row", "pair"), P())
    return jax.shard_map(
        on_device, mesh=mesh, in_specs=in_specs, out_specs=out_specs, check_vma=False
    )
```

```python
import functools

import jax
import jax.numpy as jnp
from jax import lax
from jax.experimental import pallas as pl
from jax.experimental.pallas import tpu as pltpu
from jax.sharding import PartitionSpec as P

BLOCK = 64
ITERS = 3
WIDTH = 2 * BLOCK
MESH = pl.DeviceIdType.MESH
HIGHEST = lax.Precision.HIGHEST
NEUMANN_TOL = 1e-8
X_CHIPS = 4
EARLY = 8
FACTORS = 12
PLACE_STEPS = 2


def mm(lhs, rhs, lhs_dim=1):
    return lax.dot_general(
        lhs,
        rhs,
        (((lhs_dim,), (0,)), ((), ())),
        precision=HIGHEST,
        preferred_element_type=jnp.float32,
    )


def lanes(shape):
    return lax.broadcasted_iota(jnp.int32, shape, len(shape) - 1)


def unit_mask():
    return lax.broadcasted_iota(jnp.int32, (WIDTH, WIDTH), 0) == lanes((WIDTH, WIDTH))


def skew_of(gram, unit):
    on_diag = jnp.where(unit, gram, 0.0)
    d_col = jnp.sum(on_diag, axis=1, keepdims=True)
    d_row = jnp.sum(on_diag, axis=0, keepdims=True)
    return gram * (d_col - d_row) / (2.0 * (d_col * d_col + d_row * d_row))


def series_start(state, skew, square, bound, unit):
    eye = jnp.where(unit, 1.0, 0.0).astype(jnp.float32)
    scale = 2.0 / (2.0 + bound)
    state[0:WIDTH, :] = scale * (eye - 2.0 * skew + square)
    state[WIDTH:, :] = eye - scale * (eye - square)


def series_step(state):
    both = mm(state[...], state[WIDTH:, :])
    state[0:WIDTH, :] = state[0:WIDTH, :] + both[0:WIDTH]
    state[WIDTH:, :] = both[WIDTH:]


def sweep_end(sweep, tall, state):
    v = state[0:WIDTH, :]
    if sweep == 0:
        tall[0:WIDTH, :] = mm(v, mm(tall[0:WIDTH, :], v), 0)
        tall[WIDTH:, :] = v
    elif sweep + 1 < ITERS:
        both = mm(tall[...], v)
        tall[0:WIDTH, :] = mm(v, both[0:WIDTH], 0)
        tall[WIDTH:, :] = both[WIDTH:]
    else:
        tall[WIDTH:, :] = mm(tall[WIDTH:, :], v)


def spread_kernel(
    xs, ys, zs, slots_ref, r_hbm, turned_hbm, landed, x_hbm, g_ref, ratio_ref,
    r_ref, blocks, stage, held, part, half_in, mine, z_in, full,
    tall, state, v_pair, turned, packed, sum_x, sum_y,
    out_send, out_recv, half_send, half_recv, rs_send, rs_recv, ag_send, ag_recv,
    load_sem, save_sem, v_send, v_recv, edge_send, edge_recv, g_send, g_recv,
    x_send, x_recv, y_send, y_recv,
):
    count = xs * ys
    load = pltpu.make_async_copy(r_hbm, r_ref, load_sem)
    load.start()
    me = lax.axis_index("pair")
    row = lax.axis_index("row")
    z, core = row // 2, row % 2
    other = z * 2 + (1 - core)
    rows = r_ref.shape[0]
    steps = held.shape[0]
    half = mine.shape[1]
    chunk = half // zs
    low = lanes((rows, WIDTH)) < BLOCK

    def target(k):
        return lax.rem(me + k, count)

    def z_row(k):
        return lax.rem(z + k, zs) * 2 + core

    barrier = pltpu.get_barrier_semaphore()
    y, x = me // xs, me % xs

    def x_peer(k):
        return y * xs + lax.rem(x + k, xs)

    def y_peer(k):
        return lax.rem(y + k, ys) * xs + x

    for k in range(xs):
        pl.semaphore_signal(
            barrier, inc=1, device_id={"pair": x_peer(k), "row": other}, device_id_type=MESH
        )
    for k in range(1, zs):
        pl.semaphore_signal(barrier, inc=1, device_id={"row": z_row(k)}, device_id_type=MESH)

    def greet(k, carry):
        pl.semaphore_signal(barrier, inc=1, device_id={"pair": target(k)}, device_id_type=MESH)
        return carry

    lax.fori_loop(1, count, greet, 0)

    def lift(t, carry):
        tile = r_ref[:, pl.ds(pl.multiple_of(t * WIDTH, WIDTH), WIDTH)]
        blocks[2 * t] = tile
        blocks[2 * t + 1] = pltpu.roll(tile, BLOCK, 1)
        return carry

    load.wait()
    lax.fori_loop(0, blocks.shape[0] // 2, lift, 0, unroll=8)

    def piece(group, s, i):
        slot = group * 8 + 2 * (1 + i if s else 3 * i)
        upper = blocks[slots_ref[slot]]
        lower = blocks[slots_ref[slot + 1]]
        return jnp.where(low, upper, pltpu.roll(lower, BLOCK, 1))

    def arrange(s):
        def body(k, carry):
            group = target(k)
            for i in range(2):
                stage[s, group, :, i * WIDTH : (i + 1) * WIDTH] = piece(group, s, i)
            return carry

        return body

    here = pl.ds(pl.multiple_of(me * rows, rows), rows)

    def send(s, k):
        return pltpu.make_async_remote_copy(
            src_ref=stage.at[s, target(k)],
            dst_ref=held.at[s, here],
            send_sem=out_send.at[s, k],
            recv_sem=out_recv.at[s, count - k],
            device_id={"pair": target(k)},
            device_id_type=MESH,
        )

    def start(s):
        def body(k, carry):
            send(s, k).start()
            return carry

        return body

    def both(s):
        def body(k, carry):
            arrange(s)(k, carry)
            send(s, k).start()
            return carry

        return body

    def finish(s):
        def body(k, carry):
            send(s, k).wait()
            return carry

        return body

    lax.fori_loop(1, EARLY, arrange(0), 0)
    pl.semaphore_wait(barrier, xs + zs - 1 + count - 1)
    lax.fori_loop(1, EARLY, start(0), 0)
    lax.fori_loop(EARLY, count, both(0), 0)
    for s in range(1, steps):
        lax.fori_loop(1, count, both(s), 0)
    for s in range(steps):
        for i in range(2):
            held[s, here, i * WIDTH : (i + 1) * WIDTH] = piece(me, s, i)

    def gram(s, i):
        cols = held[s, :, pl.ds(pl.multiple_of(i * WIDTH, WIDTH), WIDTH)]
        part[s, pl.ds(pl.multiple_of(i * WIDTH, WIDTH), WIDTH), :] = mm(cols, cols, 0)

    def save_turned(side):
        return pltpu.make_async_copy(turned.at[side], turned_hbm.at[side], save_sem.at[side])

    def edge_copy(side):
        return pltpu.make_async_remote_copy(
            src_ref=packed.at[side],
            dst_ref=landed.at[side],
            send_sem=edge_send.at[side],
            recv_sem=edge_recv.at[side],
            device_id={"pair": lax.rem(me + count + 2 * side - 1, count)},
            device_id_type=MESH,
        )

    unit = unit_mask()

    def rotate_edges():
        tall[0:WIDTH, :] = full[0]
        for sweep in range(ITERS):
            skew = skew_of(tall[0:WIDTH, :], unit)
            cells = jnp.sum(skew * skew, axis=0, keepdims=True)
            bound = 0.5 * jnp.sum(cells, axis=1, keepdims=True)
            series_start(state, skew, mm(skew, skew), bound, unit)

            def factor(k, carry):
                series_step(state)
                return carry

            lax.fori_loop(0, FACTORS, factor, 0)
            sweep_end(sweep, tall, state)
        v_pair[core] = tall[WIDTH:, :]
        swap = pltpu.make_async_remote_copy(
            src_ref=v_pair.at[core],
            dst_ref=v_pair.at[core],
            send_sem=v_send,
            recv_sem=v_recv,
            device_id={"row": other},
            device_id_type=MESH,
        )
        swap.start()
        swap.wait()
        edge_rows = turned.shape[1] // 2
        lane = lanes((edge_rows, WIDTH))
        for side in range(2):
            turned[side] = mm(held[0, :, side * WIDTH : (side + 1) * WIDTH], v_pair[side])
            save_turned(side).start()
            keep = (lane < BLOCK) == (side == 1)
            value = turned.at[side]
            rolled = pltpu.roll(value[edge_rows:, :], BLOCK, 1)
            packed[side] = jnp.where(keep, value[0:edge_rows, :], rolled)

    own = pl.ds(pl.multiple_of(z * chunk, chunk), chunk)
    for s in range(steps):
        lax.fori_loop(1, count, finish(s), 0)
        if s == 1:
            save = pltpu.make_async_copy(held.at[s], x_hbm, save_sem.at[2])
            save.start()
            for side in range(2):
                edge_copy(side).start()
        gram(s, 1 - core)
        swap = pltpu.make_async_remote_copy(
            src_ref=part.at[s, pl.ds(pl.multiple_of((1 - core) * half, half), half)],
            dst_ref=half_in.at[s],
            send_sem=half_send.at[s],
            recv_sem=half_recv.at[s],
            device_id={"row": other},
            device_id_type=MESH,
        )
        swap.start()
        gram(s, core)
        swap.wait()
        mine[s] = part[s, pl.ds(pl.multiple_of(core * half, half), half), :] + half_in[s]

        def scatter(k, s=s):
            at = pl.multiple_of(lax.rem(z + k, zs) * chunk, chunk)
            return pltpu.make_async_remote_copy(
                src_ref=mine.at[s, pl.ds(at, chunk)],
                dst_ref=z_in.at[s, zs - k],
                send_sem=rs_send.at[s, k],
                recv_sem=rs_recv.at[s, zs - k],
                device_id={"row": z_row(k)},
                device_id_type=MESH,
            )

        for k in range(1, zs):
            scatter(k).start()
        for k in range(1, zs):
            scatter(k).wait()
        total = mine[s, own, :]
        for k in range(1, zs):
            total = total + z_in[s, k]
        full[s, own, :] = total

        def gather(k, s=s):
            return pltpu.make_async_remote_copy(
                src_ref=full.at[s, own],
                dst_ref=full.at[s, own],
                send_sem=ag_send.at[s, k],
                recv_sem=ag_recv.at[s, zs - k],
                device_id={"row": z_row(k)},
                device_id_type=MESH,
            )

        for k in range(1, zs):
            gather(k).start()
        for k in range(1, zs):
            gather(k).wait()
        if s == 0:
            rotate_edges()

    pair_g = part.at[0]
    own_g = pl.ds(pl.multiple_of(core * half, half), half)
    pair_g[own_g, :] = full[1]
    g_swap = pltpu.make_async_remote_copy(
        src_ref=full.at[1],
        dst_ref=pair_g.at[own_g],
        send_sem=g_send,
        recv_sem=g_recv,
        device_id={"row": other},
        device_id_type=MESH,
    )

    off = jnp.zeros((1, WIDTH), jnp.float32)
    on = jnp.zeros((1, WIDTH), jnp.float32)
    for s in range(steps):
        squares = full[s] * full[s]
        off = off + jnp.sum(jnp.where(unit, 0.0, squares), axis=0, keepdims=True)
        on = on + jnp.sum(jnp.where(unit, squares, 0.0), axis=0, keepdims=True)
    tile_row = lax.broadcasted_iota(jnp.int32, (8, WIDTH), 0)
    sum_x[core, x] = jnp.where(tile_row == 0, off, jnp.where(tile_row == 1, on, 0.0))

    def x_copy(k, crossed):
        return pltpu.make_async_remote_copy(
            src_ref=sum_x.at[core, x],
            dst_ref=sum_x.at[core, x],
            send_sem=x_send.at[crossed, k],
            recv_sem=x_recv.at[crossed, (xs - k) % xs],
            device_id={"pair": x_peer(k), "row": other if crossed else row},
            device_id_type=MESH,
        )

    x_copies = [x_copy(k, crossed) for crossed in range(2) for k in range(1 - crossed, xs)]
    for copy in x_copies:
        copy.start()
    g_swap.start()
    for copy in x_copies:
        copy.wait()
    total = jnp.zeros((8, WIDTH), jnp.float32)
    for k in range(xs):
        total = total + (sum_x[0, k] + sum_x[1, k])
    sum_y[y] = total

    def y_copy(k):
        return pltpu.make_async_remote_copy(
            src_ref=sum_y.at[y],
            dst_ref=sum_y.at[y],
            send_sem=y_send.at[k],
            recv_sem=y_recv.at[ys - k],
            device_id={"pair": y_peer(k)},
            device_id_type=MESH,
        )

    for k in range(1, ys):
        y_copy(k).start()
    g_swap.wait()
    g_ref[...] = pair_g[...]
    for side in range(2):
        save_turned(side).wait()
        edge_copy(side).wait()
    save.wait()
    for k in range(1, ys):
        y_copy(k).wait()
    total = sum_y[0]
    for k in range(1, ys):
        total = total + sum_y[k]
    off = jnp.sum(total[0:1, :], axis=1, keepdims=True)
    on = jnp.sum(total[1:2, :], axis=1, keepdims=True)
    ratio_ref[...] = jnp.broadcast_to(jnp.sqrt(off / on), ratio_ref.shape)


def spread(r_factor, block_slots):
    rows, cols = r_factor.shape
    count = lax.axis_size("pair")
    xs = X_CHIPS
    ys = count // xs
    zs = lax.axis_size("row") // 2
    steps = 2
    wide = cols // count // steps
    tall_rows = rows * count
    half = WIDTH
    vmem = pl.BlockSpec(memory_space=pltpu.VMEM)
    hbm = pl.BlockSpec(memory_space=pl.ANY)
    dma = pltpu.SemaphoreType.DMA

    def f32(*shape):
        return jax.ShapeDtypeStruct(shape, jnp.float32)

    def work(*shape):
        return pltpu.VMEM(shape, jnp.float32)

    return pl.pallas_call(
        functools.partial(spread_kernel, xs, ys, zs),
        out_shape=(
            f32(2, tall_rows, WIDTH),
            f32(2, tall_rows // 2, WIDTH),
            f32(tall_rows, wide),
            f32(2 * half, WIDTH),
            f32(8, WIDTH),
        ),
        in_specs=[pl.BlockSpec(memory_space=pltpu.SMEM), hbm],
        out_specs=(hbm, hbm, hbm, vmem, vmem),
        scratch_shapes=[
            work(rows, cols),
            work(cols // BLOCK, rows, WIDTH),
            work(steps, count, rows, wide),
            work(steps, tall_rows, wide),
            work(steps, 2 * half, WIDTH),
            work(steps, half, WIDTH),
            work(steps, half, WIDTH),
            work(steps, zs, half // zs, WIDTH),
            work(steps, half, WIDTH),
            work(2 * WIDTH, WIDTH),
            work(2 * WIDTH, WIDTH),
            work(2, WIDTH, WIDTH),
            work(2, tall_rows, WIDTH),
            work(2, tall_rows // 2, WIDTH),
            work(2, xs, 8, WIDTH),
            work(ys, 8, WIDTH),
            dma((steps, count)),
            dma((steps, count)),
            dma((steps,)),
            dma((steps,)),
            dma((steps, zs)),
            dma((steps, zs)),
            dma((steps, zs)),
            dma((steps, zs)),
            dma,
            dma((3,)),
            dma,
            dma,
            dma((2,)),
            dma((2,)),
            dma,
            dma,
            dma((2, xs)),
            dma((2, xs)),
            dma((ys,)),
            dma((ys,)),
        ],
        compiler_params=pltpu.CompilerParams(collective_id=0, has_side_effects=True),
    )(block_slots, r_factor)


def rotation_kernel(g_ref, out_ref, tall, state):
    pairs = tall.shape[0]
    unit = unit_mask()
    for p in range(pairs):
        tall[p, 0:WIDTH, :] = g_ref[p * WIDTH : (p + 1) * WIDTH, :]
    for sweep in range(ITERS):
        ratio = jnp.zeros((), jnp.float32)
        for p in range(pairs):
            skew = skew_of(tall[p, 0:WIDTH, :], unit)
            square = mm(skew, skew)
            bound = jnp.max(jnp.sum(jnp.abs(square), axis=0, keepdims=True))
            series_start(state.at[p], skew, square, bound, unit)
            ratio = jnp.maximum(ratio, bound / (2.0 + bound))

        def step(carry):
            for p in range(pairs):
                series_step(state.at[p])
            return carry * carry

        lax.while_loop(lambda left: left > NEUMANN_TOL, step, ratio)
        for p in range(pairs):
            sweep_end(sweep, tall.at[p], state.at[p])
    for p in range(pairs):
        out_ref[p] = tall[p, WIDTH:, :]


def rotations(grams):
    vmem = pl.BlockSpec(memory_space=pltpu.VMEM)
    pairs = grams.shape[0] // WIDTH
    work = pltpu.VMEM((pairs, 2 * WIDTH, WIDTH), jnp.float32)
    return pl.pallas_call(
        rotation_kernel,
        out_shape=jax.ShapeDtypeStruct((pairs, WIDTH, WIDTH), jnp.float32),
        in_specs=[vmem],
        out_specs=vmem,
        scratch_shapes=[work] * 2,
    )(grams)


def place_kernel(last_pair, v_ref, x_ref, turned, landed, ratio_in, out_ref, ratio_ref):
    pair = lax.axis_index("pair")
    first, last = pair == 0, pair == last_pair
    swapped = pl.program_id(0) >= pl.num_programs(0) // 2
    low = lanes(landed.shape[1:]) < BLOCK
    from_right, from_left = landed[0], landed[1]
    from_right = jnp.where(swapped, pltpu.roll(from_right, BLOCK, 1), from_right)
    from_left = jnp.where(swapped, pltpu.roll(from_left, BLOCK, 1), from_left)
    second = mm(x_ref[:, 0:WIDTH], v_ref[0])
    third = mm(x_ref[:, WIDTH : 2 * WIDTH], v_ref[1])
    up = jnp.where(first, turned[0], from_left)
    next_up = jnp.where(first, pltpu.roll(turned[0], BLOCK, 1), turned[0])
    down = jnp.where(last, pltpu.roll(turned[1], BLOCK, 1), from_right)
    out_ref[:, 0:WIDTH] = jnp.where(low, up, second)
    out_ref[:, WIDTH : 2 * WIDTH] = jnp.where(low, next_up, third)
    out_ref[:, 2 * WIDTH : 3 * WIDTH] = jnp.where(low, second, turned[1])
    out_ref[:, 3 * WIDTH : 4 * WIDTH] = jnp.where(low, third, down)
    ratio_ref[...] = ratio_in[0:1, 0:1]


def place(turns, inner, turned, landed, ratio):
    rows, wide = inner.shape
    tile = rows // PLACE_STEPS
    return pl.pallas_call(
        functools.partial(place_kernel, lax.axis_size("pair") - 1),
        out_shape=(
            jax.ShapeDtypeStruct((rows, 2 * wide), jnp.float32),
            jax.ShapeDtypeStruct((1, 1), jnp.float32),
        ),
        grid=(PLACE_STEPS,),
        in_specs=[
            pl.BlockSpec(turns.shape, lambda g: (0, 0, 0)),
            pl.BlockSpec((tile, wide), lambda g: (g, 0)),
            pl.BlockSpec((2, tile, WIDTH), lambda g: (0, g, 0)),
            pl.BlockSpec((2, tile, WIDTH), lambda g: (0, lax.rem(g, PLACE_STEPS // 2), 0)),
            pl.BlockSpec((8, WIDTH), lambda g: (0, 0)),
        ],
        out_specs=(
            pl.BlockSpec((tile, 2 * wide), lambda g: (g, 0)),
            pl.BlockSpec((1, 1), lambda g: (0, 0)),
        ),
    )(turns, inner, turned, landed, ratio)


def on_device(r_factor, block_slots):
    turned, landed, inner, grams, ratio = spread(r_factor, block_slots)
    rotated, ratio = place(rotations(grams), inner, turned, landed, ratio)
    return (rotated, ratio.reshape(()))


def solution(mesh):
    in_specs = (P(("row", "pair"), None), P())
    out_specs = (P("row", "pair"), P())
    return jax.shard_map(
        on_device, mesh=mesh, in_specs=in_specs, out_specs=out_specs, check_vma=False
    )
```

```python
import functools

import jax
import jax.numpy as jnp
from jax import lax
from jax.experimental import pallas as pl
from jax.experimental.pallas import tpu as pltpu
from jax.sharding import PartitionSpec as P

BLOCK = 64
ITERS = 3
WIDTH = 2 * BLOCK
MESH = pl.DeviceIdType.MESH
HIGHEST = lax.Precision.HIGHEST
SERIES_TOL = 3e-8
X_CHIPS = 4
EARLY = 8
FACTORS = 8
PLACE_STEPS = 2


def mm(lhs, rhs, lhs_dim=1):
    return lax.dot_general(
        lhs,
        rhs,
        (((lhs_dim,), (0,)), ((), ())),
        precision=HIGHEST,
        preferred_element_type=jnp.float32,
    )


def lanes(shape):
    return lax.broadcasted_iota(jnp.int32, shape, len(shape) - 1)


def unit_mask():
    return lax.broadcasted_iota(jnp.int32, (WIDTH, WIDTH), 0) == lanes((WIDTH, WIDTH))


def skew_of(gram, unit):
    on_diag = jnp.where(unit, gram, 0.0)
    d_col = jnp.sum(on_diag, axis=1, keepdims=True)
    d_row = jnp.sum(on_diag, axis=0, keepdims=True)
    return gram * (d_col - d_row) / (2.0 * (d_col * d_col + d_row * d_row))


def series_start(state, skew, square, bound, unit):
    eye = jnp.where(unit, 1.0, 0.0).astype(jnp.float32)
    scale = 2.0 / (2.0 + bound)
    state[0:WIDTH, :] = scale * (eye - 2.0 * skew + square)
    state[WIDTH:, :] = eye - scale * (eye - square)


def series_step(state, reach, unit):
    square = reach * reach
    scale = 2.0 / (2.0 - square)
    both = mm(state[...], state[WIDTH:, :])
    state[0:WIDTH, :] = scale * (state[0:WIDTH, :] + both[0:WIDTH])
    state[WIDTH:, :] = scale * both[WIDTH:] + jnp.where(unit, 1.0 - scale, 0.0)
    return square / (2.0 - square)


def sweep_end(sweep, tall, state):
    v = state[0:WIDTH, :]
    if sweep == 0:
        tall[0:WIDTH, :] = mm(v, mm(tall[0:WIDTH, :], v), 0)
        tall[WIDTH:, :] = v
    elif sweep + 1 < ITERS:
        both = mm(tall[...], v)
        tall[0:WIDTH, :] = mm(v, both[0:WIDTH], 0)
        tall[WIDTH:, :] = both[WIDTH:]
    else:
        tall[WIDTH:, :] = mm(tall[WIDTH:, :], v)


def spread_kernel(
    xs, ys, zs, slots_ref, r_hbm, turned_hbm, landed, x_hbm, g_ref, ratio_ref,
    r_ref, blocks, stage, held, part, half_in, mine, z_in, full,
    tall, state, v_pair, turned, packed, sum_x, sum_y,
    out_send, out_recv, half_send, half_recv, rs_send, rs_recv, ag_send, ag_recv,
    load_sem, save_sem, v_send, v_recv, edge_send, edge_recv, g_send, g_recv,
    x_send, x_recv, y_send, y_recv,
):
    count = xs * ys
    load = pltpu.make_async_copy(r_hbm, r_ref, load_sem)
    load.start()
    me = lax.axis_index("pair")
    row = lax.axis_index("row")
    z, core = row // 2, row % 2
    other = z * 2 + (1 - core)
    rows = r_ref.shape[0]
    steps = held.shape[0]
    half = mine.shape[1]
    chunk = half // zs
    low = lanes((rows, WIDTH)) < BLOCK

    def target(k):
        return lax.rem(me + k, count)

    def z_row(k):
        return lax.rem(z + k, zs) * 2 + core

    barrier = pltpu.get_barrier_semaphore()
    y, x = me // xs, me % xs

    def x_peer(k):
        return y * xs + lax.rem(x + k, xs)

    def y_peer(k):
        return lax.rem(y + k, ys) * xs + x

    for k in range(xs):
        pl.semaphore_signal(
            barrier, inc=1, device_id={"pair": x_peer(k), "row": other}, device_id_type=MESH
        )
    for k in range(1, zs):
        pl.semaphore_signal(barrier, inc=1, device_id={"row": z_row(k)}, device_id_type=MESH)

    def greet(k, carry):
        pl.semaphore_signal(barrier, inc=1, device_id={"pair": target(k)}, device_id_type=MESH)
        return carry

    lax.fori_loop(1, count, greet, 0)

    def lift(t, carry):
        tile = r_ref[:, pl.ds(pl.multiple_of(t * WIDTH, WIDTH), WIDTH)]
        blocks[2 * t] = tile
        blocks[2 * t + 1] = pltpu.roll(tile, BLOCK, 1)
        return carry

    load.wait()
    lax.fori_loop(0, blocks.shape[0] // 2, lift, 0, unroll=8)

    def piece(group, s, i):
        slot = group * 8 + 2 * (1 + i if s else 3 * i)
        upper = blocks[slots_ref[slot]]
        lower = blocks[slots_ref[slot + 1]]
        return jnp.where(low, upper, pltpu.roll(lower, BLOCK, 1))

    def arrange(s):
        def body(k, carry):
            group = target(k)
            for i in range(2):
                stage[s, group, :, i * WIDTH : (i + 1) * WIDTH] = piece(group, s, i)
            return carry

        return body

    here = pl.ds(pl.multiple_of(me * rows, rows), rows)

    def send(s, k):
        return pltpu.make_async_remote_copy(
            src_ref=stage.at[s, target(k)],
            dst_ref=held.at[s, here],
            send_sem=out_send.at[s, k],
            recv_sem=out_recv.at[s, count - k],
            device_id={"pair": target(k)},
            device_id_type=MESH,
        )

    def start(s):
        def body(k, carry):
            send(s, k).start()
            return carry

        return body

    def both(s):
        def body(k, carry):
            arrange(s)(k, carry)
            send(s, k).start()
            return carry

        return body

    def finish(s):
        def body(k, carry):
            send(s, k).wait_recv()
            if s == 1:
                send(s, k).wait_send()
            return carry

        return body

    lax.fori_loop(1, EARLY, arrange(0), 0)
    pl.semaphore_wait(barrier, xs + zs - 1 + count - 1)
    lax.fori_loop(1, EARLY, start(0), 0)
    lax.fori_loop(EARLY, count, both(0), 0)
    for s in range(steps):
        for i in range(2):
            held[s, here, i * WIDTH : (i + 1) * WIDTH] = piece(me, s, i)

    def follow(k, carry):
        arrange(1)(k, carry)
        send(0, k).wait_send()
        send(1, k).start()
        return carry

    lax.fori_loop(1, count, follow, 0)

    def gram(s, i):
        cols = held[s, :, pl.ds(pl.multiple_of(i * WIDTH, WIDTH), WIDTH)]
        part[s, pl.ds(pl.multiple_of(i * WIDTH, WIDTH), WIDTH), :] = mm(cols, cols, 0)

    def save_turned(side):
        return pltpu.make_async_copy(turned.at[side], turned_hbm.at[side], save_sem.at[side])

    def edge_copy(side):
        return pltpu.make_async_remote_copy(
            src_ref=packed.at[side],
            dst_ref=landed.at[side],
            send_sem=edge_send.at[side],
            recv_sem=edge_recv.at[side],
            device_id={"pair": lax.rem(me + count + 2 * side - 1, count)},
            device_id_type=MESH,
        )

    unit = unit_mask()

    def rotate_edges():
        tall[0:WIDTH, :] = full[0]
        for sweep in range(ITERS):
            skew = skew_of(tall[0:WIDTH, :], unit)
            cells = jnp.sum(skew * skew, axis=0, keepdims=True)
            bound = 0.5 * jnp.sum(cells, axis=1, keepdims=True)
            series_start(state, skew, mm(skew, skew), bound, unit)

            def factor(k, reach):
                return series_step(state, reach, unit)

            lax.fori_loop(0, FACTORS, factor, bound / (2.0 + bound))
            sweep_end(sweep, tall, state)
        v_pair[core] = tall[WIDTH:, :]
        swap = pltpu.make_async_remote_copy(
            src_ref=v_pair.at[core],
            dst_ref=v_pair.at[core],
            send_sem=v_send,
            recv_sem=v_recv,
            device_id={"row": other},
            device_id_type=MESH,
        )
        swap.start()
        swap.wait()
        edge_rows = turned.shape[1] // 2
        lane = lanes((edge_rows, WIDTH))
        for side in range(2):
            turned[side] = mm(held[0, :, side * WIDTH : (side + 1) * WIDTH], v_pair[side])
            save_turned(side).start()
            keep = (lane < BLOCK) == (side == 1)
            value = turned.at[side]
            rolled = pltpu.roll(value[edge_rows:, :], BLOCK, 1)
            packed[side] = jnp.where(keep, value[0:edge_rows, :], rolled)

    own = pl.ds(pl.multiple_of(z * chunk, chunk), chunk)
    for s in range(steps):
        lax.fori_loop(1, count, finish(s), 0)
        if s == 1:
            save = pltpu.make_async_copy(held.at[s], x_hbm, save_sem.at[2])
            save.start()
            for side in range(2):
                edge_copy(side).start()
        gram(s, 1 - core)
        swap = pltpu.make_async_remote_copy(
            src_ref=part.at[s, pl.ds(pl.multiple_of((1 - core) * half, half), half)],
            dst_ref=half_in.at[s],
            send_sem=half_send.at[s],
            recv_sem=half_recv.at[s],
            device_id={"row": other},
            device_id_type=MESH,
        )
        swap.start()
        gram(s, core)
        swap.wait()
        mine[s] = part[s, pl.ds(pl.multiple_of(core * half, half), half), :] + half_in[s]

        def scatter(k, s=s):
            at = pl.multiple_of(lax.rem(z + k, zs) * chunk, chunk)
            return pltpu.make_async_remote_copy(
                src_ref=mine.at[s, pl.ds(at, chunk)],
                dst_ref=z_in.at[s, zs - k],
                send_sem=rs_send.at[s, k],
                recv_sem=rs_recv.at[s, zs - k],
                device_id={"row": z_row(k)},
                device_id_type=MESH,
            )

        for k in range(1, zs):
            scatter(k).start()
        for k in range(1, zs):
            scatter(k).wait()
        total = mine[s, own, :]
        for k in range(1, zs):
            total = total + z_in[s, k]
        full[s, own, :] = total

        def gather(k, s=s):
            return pltpu.make_async_remote_copy(
                src_ref=full.at[s, own],
                dst_ref=full.at[s, own],
                send_sem=ag_send.at[s, k],
                recv_sem=ag_recv.at[s, zs - k],
                device_id={"row": z_row(k)},
                device_id_type=MESH,
            )

        for k in range(1, zs):
            gather(k).start()
        for k in range(1, zs):
            gather(k).wait()
        if s == 0:
            rotate_edges()

    pair_g = part.at[0]
    own_g = pl.ds(pl.multiple_of(core * half, half), half)
    pair_g[own_g, :] = full[1]
    g_swap = pltpu.make_async_remote_copy(
        src_ref=full.at[1],
        dst_ref=pair_g.at[own_g],
        send_sem=g_send,
        recv_sem=g_recv,
        device_id={"row": other},
        device_id_type=MESH,
    )

    off = jnp.zeros((1, WIDTH), jnp.float32)
    on = jnp.zeros((1, WIDTH), jnp.float32)
    for s in range(steps):
        squares = full[s] * full[s]
        off = off + jnp.sum(jnp.where(unit, 0.0, squares), axis=0, keepdims=True)
        on = on + jnp.sum(jnp.where(unit, squares, 0.0), axis=0, keepdims=True)
    tile_row = lax.broadcasted_iota(jnp.int32, (8, WIDTH), 0)
    sum_x[core, x] = jnp.where(tile_row == 0, off, jnp.where(tile_row == 1, on, 0.0))

    def x_copy(k, crossed):
        return pltpu.make_async_remote_copy(
            src_ref=sum_x.at[core, x],
            dst_ref=sum_x.at[core, x],
            send_sem=x_send.at[crossed, k],
            recv_sem=x_recv.at[crossed, (xs - k) % xs],
            device_id={"pair": x_peer(k), "row": other if crossed else row},
            device_id_type=MESH,
        )

    x_copies = [x_copy(k, crossed) for crossed in range(2) for k in range(1 - crossed, xs)]
    for copy in x_copies:
        copy.start()
    g_swap.start()
    for copy in x_copies:
        copy.wait()
    total = jnp.zeros((8, WIDTH), jnp.float32)
    for k in range(xs):
        total = total + (sum_x[0, k] + sum_x[1, k])
    sum_y[y] = total

    def y_copy(k):
        return pltpu.make_async_remote_copy(
            src_ref=sum_y.at[y],
            dst_ref=sum_y.at[y],
            send_sem=y_send.at[k],
            recv_sem=y_recv.at[ys - k],
            device_id={"pair": y_peer(k)},
            device_id_type=MESH,
        )

    for k in range(1, ys):
        y_copy(k).start()
    g_swap.wait()
    g_ref[...] = pair_g[...]
    for side in range(2):
        save_turned(side).wait()
        edge_copy(side).wait()
    save.wait()
    for k in range(1, ys):
        y_copy(k).wait()
    total = sum_y[0]
    for k in range(1, ys):
        total = total + sum_y[k]
    off = jnp.sum(total[0:1, :], axis=1, keepdims=True)
    on = jnp.sum(total[1:2, :], axis=1, keepdims=True)
    ratio_ref[...] = jnp.broadcast_to(jnp.sqrt(off / on), ratio_ref.shape)


def spread(r_factor, block_slots):
    rows, cols = r_factor.shape
    count = lax.axis_size("pair")
    xs = X_CHIPS
    ys = count // xs
    zs = lax.axis_size("row") // 2
    steps = 2
    wide = cols // count // steps
    tall_rows = rows * count
    half = WIDTH
    vmem = pl.BlockSpec(memory_space=pltpu.VMEM)
    hbm = pl.BlockSpec(memory_space=pl.ANY)
    dma = pltpu.SemaphoreType.DMA

    def f32(*shape):
        return jax.ShapeDtypeStruct(shape, jnp.float32)

    def work(*shape):
        return pltpu.VMEM(shape, jnp.float32)

    return pl.pallas_call(
        functools.partial(spread_kernel, xs, ys, zs),
        out_shape=(
            f32(2, tall_rows, WIDTH),
            f32(2, tall_rows // 2, WIDTH),
            f32(tall_rows, wide),
            f32(2 * half, WIDTH),
            f32(8, WIDTH),
        ),
        in_specs=[pl.BlockSpec(memory_space=pltpu.SMEM), hbm],
        out_specs=(hbm, hbm, hbm, vmem, vmem),
        scratch_shapes=[
            work(rows, cols),
            work(cols // BLOCK, rows, WIDTH),
            work(steps, count, rows, wide),
            work(steps, tall_rows, wide),
            work(steps, 2 * half, WIDTH),
            work(steps, half, WIDTH),
            work(steps, half, WIDTH),
            work(steps, zs, half // zs, WIDTH),
            work(steps, half, WIDTH),
            work(2 * WIDTH, WIDTH),
            work(2 * WIDTH, WIDTH),
            work(2, WIDTH, WIDTH),
            work(2, tall_rows, WIDTH),
            work(2, tall_rows // 2, WIDTH),
            work(2, xs, 8, WIDTH),
            work(ys, 8, WIDTH),
            dma((steps, count)),
            dma((steps, count)),
            dma((steps,)),
            dma((steps,)),
            dma((steps, zs)),
            dma((steps, zs)),
            dma((steps, zs)),
            dma((steps, zs)),
            dma,
            dma((3,)),
            dma,
            dma,
            dma((2,)),
            dma((2,)),
            dma,
            dma,
            dma((2, xs)),
            dma((2, xs)),
            dma((ys,)),
            dma((ys,)),
        ],
        compiler_params=pltpu.CompilerParams(collective_id=0, has_side_effects=True),
    )(block_slots, r_factor)


def rotation_kernel(g_ref, out_ref, tall, state):
    pairs = tall.shape[0]
    unit = unit_mask()
    for p in range(pairs):
        tall[p, 0:WIDTH, :] = g_ref[p * WIDTH : (p + 1) * WIDTH, :]
    for sweep in range(ITERS):
        most = jnp.zeros((), jnp.float32)
        work = []
        for p in range(pairs):
            skew = skew_of(tall[p, 0:WIDTH, :], unit)
            square = mm(skew, skew)
            bound = jnp.max(jnp.sum(jnp.abs(square), axis=0, keepdims=True))
            work.append((skew, square))
            most = jnp.maximum(most, bound)
        for p in range(pairs):
            series_start(state.at[p], *work[p], most, unit)

        def step(reach):
            for p in range(pairs):
                after = series_step(state.at[p], reach, unit)
            return after

        lax.while_loop(lambda reach: reach > SERIES_TOL, step, most / (2.0 + most))
        for p in range(pairs):
            sweep_end(sweep, tall.at[p], state.at[p])
    for p in range(pairs):
        out_ref[p] = tall[p, WIDTH:, :]


def rotations(grams):
    vmem = pl.BlockSpec(memory_space=pltpu.VMEM)
    pairs = grams.shape[0] // WIDTH
    work = pltpu.VMEM((pairs, 2 * WIDTH, WIDTH), jnp.float32)
    return pl.pallas_call(
        rotation_kernel,
        out_shape=jax.ShapeDtypeStruct((pairs, WIDTH, WIDTH), jnp.float32),
        in_specs=[vmem],
        out_specs=vmem,
        scratch_shapes=[work] * 2,
    )(grams)


def place_kernel(last_pair, v_ref, x_ref, turned, landed, ratio_in, out_ref, ratio_ref):
    pair = lax.axis_index("pair")
    first, last = pair == 0, pair == last_pair
    swapped = pl.program_id(0) >= pl.num_programs(0) // 2
    low = lanes(landed.shape[1:]) < BLOCK
    from_right, from_left = landed[0], landed[1]
    from_right = jnp.where(swapped, pltpu.roll(from_right, BLOCK, 1), from_right)
    from_left = jnp.where(swapped, pltpu.roll(from_left, BLOCK, 1), from_left)
    second = mm(x_ref[:, 0:WIDTH], v_ref[0])
    third = mm(x_ref[:, WIDTH : 2 * WIDTH], v_ref[1])
    up = jnp.where(first, turned[0], from_left)
    next_up = jnp.where(first, pltpu.roll(turned[0], BLOCK, 1), turned[0])
    down = jnp.where(last, pltpu.roll(turned[1], BLOCK, 1), from_right)
    out_ref[:, 0:WIDTH] = jnp.where(low, up, second)
    out_ref[:, WIDTH : 2 * WIDTH] = jnp.where(low, next_up, third)
    out_ref[:, 2 * WIDTH : 3 * WIDTH] = jnp.where(low, second, turned[1])
    out_ref[:, 3 * WIDTH : 4 * WIDTH] = jnp.where(low, third, down)
    ratio_ref[...] = ratio_in[0:1, 0:1]


def place(turns, inner, turned, landed, ratio):
    rows, wide = inner.shape
    tile = rows // PLACE_STEPS
    return pl.pallas_call(
        functools.partial(place_kernel, lax.axis_size("pair") - 1),
        out_shape=(
            jax.ShapeDtypeStruct((rows, 2 * wide), jnp.float32),
            jax.ShapeDtypeStruct((1, 1), jnp.float32),
        ),
        grid=(PLACE_STEPS,),
        in_specs=[
            pl.BlockSpec(turns.shape, lambda g: (0, 0, 0)),
            pl.BlockSpec((tile, wide), lambda g: (g, 0)),
            pl.BlockSpec((2, tile, WIDTH), lambda g: (0, g, 0)),
            pl.BlockSpec((2, tile, WIDTH), lambda g: (0, lax.rem(g, PLACE_STEPS // 2), 0)),
            pl.BlockSpec((8, WIDTH), lambda g: (0, 0)),
        ],
        out_specs=(
            pl.BlockSpec((tile, 2 * wide), lambda g: (g, 0)),
            pl.BlockSpec((1, 1), lambda g: (0, 0)),
        ),
    )(turns, inner, turned, landed, ratio)


def on_device(r_factor, block_slots):
    turned, landed, inner, grams, ratio = spread(r_factor, block_slots)
    rotated, ratio = place(rotations(grams), inner, turned, landed, ratio)
    return (rotated, ratio.reshape(()))


def solution(mesh):
    in_specs = (P(("row", "pair"), None), P())
    out_specs = (P("row", "pair"), P())
    return jax.shard_map(
        on_device, mesh=mesh, in_specs=in_specs, out_specs=out_specs, check_vma=False
    )
```

```python
import functools

import jax
import jax.numpy as jnp
from jax import lax
from jax.experimental import pallas as pl
from jax.experimental.pallas import tpu as pltpu
from jax.sharding import PartitionSpec as P

BLOCK = 64
ITERS = 3
WIDTH = 2 * BLOCK
MESH = pl.DeviceIdType.MESH
HIGHEST = lax.Precision.HIGHEST
SERIES_TOL = 3e-8
X_CHIPS = 4
EARLY = 8
FACTORS = 8
BEFORE = 2
PLACE_STEPS = 2


def mm(lhs, rhs, lhs_dim=1):
    return lax.dot_general(
        lhs,
        rhs,
        (((lhs_dim,), (0,)), ((), ())),
        precision=HIGHEST,
        preferred_element_type=jnp.float32,
    )


def lanes(shape):
    return lax.broadcasted_iota(jnp.int32, shape, len(shape) - 1)


def unit_mask():
    return lax.broadcasted_iota(jnp.int32, (WIDTH, WIDTH), 0) == lanes((WIDTH, WIDTH))


def skew_of(gram, unit):
    on_diag = jnp.where(unit, gram, 0.0)
    d_col = jnp.sum(on_diag, axis=1, keepdims=True)
    d_row = jnp.sum(on_diag, axis=0, keepdims=True)
    return gram * (d_col - d_row) / (2.0 * (d_col * d_col + d_row * d_row))


def series_start(state, skew, square, bound, unit):
    eye = jnp.where(unit, 1.0, 0.0).astype(jnp.float32)
    scale = 2.0 / (2.0 + bound)
    state[0:WIDTH, :] = scale * (eye - 2.0 * skew + square)
    state[WIDTH:, :] = eye - scale * (eye - square)


def series_step(state, reach, unit):
    square = reach * reach
    scale = 2.0 / (2.0 - square)
    both = mm(state[...], state[WIDTH:, :])
    state[0:WIDTH, :] = scale * (state[0:WIDTH, :] + both[0:WIDTH])
    state[WIDTH:, :] = scale * both[WIDTH:] + jnp.where(unit, 1.0 - scale, 0.0)
    return square / (2.0 - square)


def sweep_end(sweep, tall, state):
    v = state[0:WIDTH, :]
    if sweep == 0:
        tall[0:WIDTH, :] = mm(v, mm(tall[0:WIDTH, :], v), 0)
        tall[WIDTH:, :] = v
    elif sweep + 1 < ITERS:
        both = mm(tall[...], v)
        tall[0:WIDTH, :] = mm(v, both[0:WIDTH], 0)
        tall[WIDTH:, :] = both[WIDTH:]
    else:
        tall[WIDTH:, :] = mm(tall[WIDTH:, :], v)


def spread_kernel(
    xs, ys, zs, slots_ref, r_hbm, turned_hbm, landed, x_hbm, g_ref, ratio_ref,
    r_ref, blocks, stage, held, part, half_in, mine, z_in, full,
    tall, state, v_pair, turned, packed, sum_x, sum_y,
    out_send, out_recv, half_send, half_recv, rs_send, rs_recv, ag_send, ag_recv,
    load_sem, save_sem, v_send, v_recv, edge_send, edge_recv, g_send, g_recv,
    x_send, x_recv, y_send, y_recv,
):
    count = xs * ys
    load = pltpu.make_async_copy(r_hbm, r_ref, load_sem)
    load.start()
    me = lax.axis_index("pair")
    row = lax.axis_index("row")
    z, core = row // 2, row % 2
    other = z * 2 + (1 - core)
    rows = r_ref.shape[0]
    steps = held.shape[0]
    half = mine.shape[1]
    chunk = half // zs
    low = lanes((rows, WIDTH)) < BLOCK

    def target(k):
        return lax.rem(me + k, count)

    def z_row(k):
        return lax.rem(z + k, zs) * 2 + core

    barrier = pltpu.get_barrier_semaphore()
    y, x = me // xs, me % xs

    def x_peer(k):
        return y * xs + lax.rem(x + k, xs)

    def y_peer(k):
        return lax.rem(y + k, ys) * xs + x

    for k in range(xs):
        pl.semaphore_signal(
            barrier, inc=1, device_id={"pair": x_peer(k), "row": other}, device_id_type=MESH
        )
    for k in range(1, zs):
        pl.semaphore_signal(barrier, inc=1, device_id={"row": z_row(k)}, device_id_type=MESH)

    def greet(k, carry):
        pl.semaphore_signal(barrier, inc=1, device_id={"pair": target(k)}, device_id_type=MESH)
        return carry

    lax.fori_loop(1, count, greet, 0)

    def lift(t, carry):
        tile = r_ref[:, pl.ds(pl.multiple_of(t * WIDTH, WIDTH), WIDTH)]
        blocks[2 * t] = tile
        blocks[2 * t + 1] = pltpu.roll(tile, BLOCK, 1)
        return carry

    load.wait()
    lax.fori_loop(0, blocks.shape[0] // 2, lift, 0, unroll=8)

    def piece(group, s, i):
        slot = group * 8 + 2 * (1 + i if s else 3 * i)
        upper = blocks[slots_ref[slot]]
        lower = blocks[slots_ref[slot + 1]]
        return jnp.where(low, upper, pltpu.roll(lower, BLOCK, 1))

    def arrange(s):
        def body(k, carry):
            group = target(k)
            for i in range(2):
                stage[s, group, :, i * WIDTH : (i + 1) * WIDTH] = piece(group, s, i)
            return carry

        return body

    here = pl.ds(pl.multiple_of(me * rows, rows), rows)

    def send(s, k):
        return pltpu.make_async_remote_copy(
            src_ref=stage.at[s, target(k)],
            dst_ref=held.at[s, here],
            send_sem=out_send.at[s, k],
            recv_sem=out_recv.at[s, count - k],
            device_id={"pair": target(k)},
            device_id_type=MESH,
        )

    def start(s):
        def body(k, carry):
            send(s, k).start()
            return carry

        return body

    def both(s):
        def body(k, carry):
            arrange(s)(k, carry)
            send(s, k).start()
            return carry

        return body

    def finish(s):
        def body(k, carry):
            send(s, k).wait_recv()
            if s == 1:
                send(s, k).wait_send()
            return carry

        return body

    lax.fori_loop(1, EARLY, arrange(0), 0)
    pl.semaphore_wait(barrier, xs + zs - 1 + count - 1)
    lax.fori_loop(1, EARLY, start(0), 0)
    lax.fori_loop(EARLY, count, both(0), 0)
    for s in range(steps):
        for i in range(2):
            held[s, here, i * WIDTH : (i + 1) * WIDTH] = piece(me, s, i)

    def follow(k, carry):
        arrange(1)(k, carry)
        send(0, k).wait_send()
        send(1, k).start()
        return carry

    lax.fori_loop(1, count, follow, 0)

    def gram(s, i):
        cols = held[s, :, pl.ds(pl.multiple_of(i * WIDTH, WIDTH), WIDTH)]
        part[s, pl.ds(pl.multiple_of(i * WIDTH, WIDTH), WIDTH), :] = mm(cols, cols, 0)

    def save_turned(side):
        return pltpu.make_async_copy(turned.at[side], turned_hbm.at[side], save_sem.at[side])

    def edge_copy(side):
        return pltpu.make_async_remote_copy(
            src_ref=packed.at[side],
            dst_ref=landed.at[side],
            send_sem=edge_send.at[side],
            recv_sem=edge_recv.at[side],
            device_id={"pair": lax.rem(me + count + 2 * side - 1, count)},
            device_id_type=MESH,
        )

    unit = unit_mask()

    def edge_sweep(sweep):
        if sweep == 0:
            tall[0:WIDTH, :] = full[0]
        skew = skew_of(tall[0:WIDTH, :], unit)
        cells = jnp.sum(skew * skew, axis=0, keepdims=True)
        bound = 0.5 * jnp.sum(cells, axis=1, keepdims=True)
        series_start(state, skew, mm(skew, skew), bound, unit)

        def factor(k, reach):
            return series_step(state, reach, unit)

        lax.fori_loop(0, FACTORS, factor, bound / (2.0 + bound))
        sweep_end(sweep, tall, state)

    v_swap = pltpu.make_async_remote_copy(
        src_ref=v_pair.at[core],
        dst_ref=v_pair.at[core],
        send_sem=v_send,
        recv_sem=v_recv,
        device_id={"row": other},
        device_id_type=MESH,
    )

    def send_edges():
        edge_rows = turned.shape[1] // 2
        lane = lanes((edge_rows, WIDTH))
        for side in range(2):
            turned[side] = mm(held[0, :, side * WIDTH : (side + 1) * WIDTH], v_pair[side])
            save_turned(side).start()
            keep = (lane < BLOCK) == (side == 1)
            value = turned.at[side]
            rolled = pltpu.roll(value[edge_rows:, :], BLOCK, 1)
            packed[side] = jnp.where(keep, value[0:edge_rows, :], rolled)
            edge_copy(side).start()

    own = pl.ds(pl.multiple_of(z * chunk, chunk), chunk)
    for s in range(steps):
        lax.fori_loop(1, count, finish(s), 0)
        if s == 1:
            save = pltpu.make_async_copy(held.at[s], x_hbm, save_sem.at[2])
            save.start()
        gram(s, 1 - core)
        swap = pltpu.make_async_remote_copy(
            src_ref=part.at[s, pl.ds(pl.multiple_of((1 - core) * half, half), half)],
            dst_ref=half_in.at[s],
            send_sem=half_send.at[s],
            recv_sem=half_recv.at[s],
            device_id={"row": other},
            device_id_type=MESH,
        )
        swap.start()
        gram(s, core)
        swap.wait()
        mine[s] = part[s, pl.ds(pl.multiple_of(core * half, half), half), :] + half_in[s]

        def scatter(k, s=s):
            at = pl.multiple_of(lax.rem(z + k, zs) * chunk, chunk)
            return pltpu.make_async_remote_copy(
                src_ref=mine.at[s, pl.ds(at, chunk)],
                dst_ref=z_in.at[s, zs - k],
                send_sem=rs_send.at[s, k],
                recv_sem=rs_recv.at[s, zs - k],
                device_id={"row": z_row(k)},
                device_id_type=MESH,
            )

        for k in range(1, zs):
            scatter(k).start()
        if s == 1:
            for sweep in range(BEFORE, ITERS):
                edge_sweep(sweep)
            v_pair[core] = tall[WIDTH:, :]
        for k in range(1, zs):
            scatter(k).wait()
        total = mine[s, own, :]
        for k in range(1, zs):
            total = total + z_in[s, k]
        full[s, own, :] = total

        def gather(k, s=s):
            return pltpu.make_async_remote_copy(
                src_ref=full.at[s, own],
                dst_ref=full.at[s, own],
                send_sem=ag_send.at[s, k],
                recv_sem=ag_recv.at[s, zs - k],
                device_id={"row": z_row(k)},
                device_id_type=MESH,
            )

        for k in range(1, zs):
            gather(k).start()
        if s == 1:
            v_swap.start()
            v_swap.wait()
            send_edges()
        for k in range(1, zs):
            gather(k).wait()
        if s == 0:
            for sweep in range(BEFORE):
                edge_sweep(sweep)

    pair_g = part.at[0]
    own_g = pl.ds(pl.multiple_of(core * half, half), half)
    pair_g[own_g, :] = full[1]
    g_swap = pltpu.make_async_remote_copy(
        src_ref=full.at[1],
        dst_ref=pair_g.at[own_g],
        send_sem=g_send,
        recv_sem=g_recv,
        device_id={"row": other},
        device_id_type=MESH,
    )

    off = jnp.zeros((1, WIDTH), jnp.float32)
    on = jnp.zeros((1, WIDTH), jnp.float32)
    for s in range(steps):
        squares = full[s] * full[s]
        off = off + jnp.sum(jnp.where(unit, 0.0, squares), axis=0, keepdims=True)
        on = on + jnp.sum(jnp.where(unit, squares, 0.0), axis=0, keepdims=True)
    tile_row = lax.broadcasted_iota(jnp.int32, (8, WIDTH), 0)
    sum_x[core, x] = jnp.where(tile_row == 0, off, jnp.where(tile_row == 1, on, 0.0))

    def x_copy(k, crossed):
        return pltpu.make_async_remote_copy(
            src_ref=sum_x.at[core, x],
            dst_ref=sum_x.at[core, x],
            send_sem=x_send.at[crossed, k],
            recv_sem=x_recv.at[crossed, (xs - k) % xs],
            device_id={"pair": x_peer(k), "row": other if crossed else row},
            device_id_type=MESH,
        )

    x_copies = [x_copy(k, crossed) for crossed in range(2) for k in range(1 - crossed, xs)]
    for copy in x_copies:
        copy.start()
    g_swap.start()
    for copy in x_copies:
        copy.wait()
    total = jnp.zeros((8, WIDTH), jnp.float32)
    for k in range(xs):
        total = total + (sum_x[0, k] + sum_x[1, k])
    sum_y[y] = total

    def y_copy(k):
        return pltpu.make_async_remote_copy(
            src_ref=sum_y.at[y],
            dst_ref=sum_y.at[y],
            send_sem=y_send.at[k],
            recv_sem=y_recv.at[ys - k],
            device_id={"pair": y_peer(k)},
            device_id_type=MESH,
        )

    for k in range(1, ys):
        y_copy(k).start()
    g_swap.wait()
    g_ref[...] = pair_g[...]
    for side in range(2):
        save_turned(side).wait()
        edge_copy(side).wait()
    save.wait()
    for k in range(1, ys):
        y_copy(k).wait()
    total = sum_y[0]
    for k in range(1, ys):
        total = total + sum_y[k]
    off = jnp.sum(total[0:1, :], axis=1, keepdims=True)
    on = jnp.sum(total[1:2, :], axis=1, keepdims=True)
    ratio_ref[...] = jnp.broadcast_to(jnp.sqrt(off / on), ratio_ref.shape)


def spread(r_factor, block_slots):
    rows, cols = r_factor.shape
    count = lax.axis_size("pair")
    xs = X_CHIPS
    ys = count // xs
    zs = lax.axis_size("row") // 2
    steps = 2
    wide = cols // count // steps
    tall_rows = rows * count
    half = WIDTH
    vmem = pl.BlockSpec(memory_space=pltpu.VMEM)
    hbm = pl.BlockSpec(memory_space=pl.ANY)
    dma = pltpu.SemaphoreType.DMA

    def f32(*shape):
        return jax.ShapeDtypeStruct(shape, jnp.float32)

    def work(*shape):
        return pltpu.VMEM(shape, jnp.float32)

    return pl.pallas_call(
        functools.partial(spread_kernel, xs, ys, zs),
        out_shape=(
            f32(2, tall_rows, WIDTH),
            f32(2, tall_rows // 2, WIDTH),
            f32(tall_rows, wide),
            f32(2 * half, WIDTH),
            f32(8, WIDTH),
        ),
        in_specs=[pl.BlockSpec(memory_space=pltpu.SMEM), hbm],
        out_specs=(hbm, hbm, hbm, vmem, vmem),
        scratch_shapes=[
            work(rows, cols),
            work(cols // BLOCK, rows, WIDTH),
            work(steps, count, rows, wide),
            work(steps, tall_rows, wide),
            work(steps, 2 * half, WIDTH),
            work(steps, half, WIDTH),
            work(steps, half, WIDTH),
            work(steps, zs, half // zs, WIDTH),
            work(steps, half, WIDTH),
            work(2 * WIDTH, WIDTH),
            work(2 * WIDTH, WIDTH),
            work(2, WIDTH, WIDTH),
            work(2, tall_rows, WIDTH),
            work(2, tall_rows // 2, WIDTH),
            work(2, xs, 8, WIDTH),
            work(ys, 8, WIDTH),
            dma((steps, count)),
            dma((steps, count)),
            dma((steps,)),
            dma((steps,)),
            dma((steps, zs)),
            dma((steps, zs)),
            dma((steps, zs)),
            dma((steps, zs)),
            dma,
            dma((3,)),
            dma,
            dma,
            dma((2,)),
            dma((2,)),
            dma,
            dma,
            dma((2, xs)),
            dma((2, xs)),
            dma((ys,)),
            dma((ys,)),
        ],
        compiler_params=pltpu.CompilerParams(collective_id=0, has_side_effects=True),
    )(block_slots, r_factor)


def rotation_kernel(g_ref, out_ref, tall, state):
    pairs = tall.shape[0]
    unit = unit_mask()
    for p in range(pairs):
        tall[p, 0:WIDTH, :] = g_ref[p * WIDTH : (p + 1) * WIDTH, :]
    for sweep in range(ITERS):
        most = jnp.zeros((), jnp.float32)
        work = []
        for p in range(pairs):
            skew = skew_of(tall[p, 0:WIDTH, :], unit)
            square = mm(skew, skew)
            bound = jnp.max(jnp.sum(jnp.abs(square), axis=0, keepdims=True))
            work.append((skew, square))
            most = jnp.maximum(most, bound)
        for p in range(pairs):
            series_start(state.at[p], *work[p], most, unit)

        def step(reach):
            for p in range(pairs):
                after = series_step(state.at[p], reach, unit)
            return after

        lax.while_loop(lambda reach: reach > SERIES_TOL, step, most / (2.0 + most))
        for p in range(pairs):
            sweep_end(sweep, tall.at[p], state.at[p])
    for p in range(pairs):
        out_ref[p] = tall[p, WIDTH:, :]


def rotations(grams):
    vmem = pl.BlockSpec(memory_space=pltpu.VMEM)
    pairs = grams.shape[0] // WIDTH
    work = pltpu.VMEM((pairs, 2 * WIDTH, WIDTH), jnp.float32)
    return pl.pallas_call(
        rotation_kernel,
        out_shape=jax.ShapeDtypeStruct((pairs, WIDTH, WIDTH), jnp.float32),
        in_specs=[vmem],
        out_specs=vmem,
        scratch_shapes=[work] * 2,
    )(grams)


def place_kernel(last_pair, v_ref, x_ref, turned, landed, ratio_in, out_ref, ratio_ref):
    pair = lax.axis_index("pair")
    first, last = pair == 0, pair == last_pair
    swapped = pl.program_id(0) >= pl.num_programs(0) // 2
    low = lanes(landed.shape[1:]) < BLOCK
    from_right, from_left = landed[0], landed[1]
    from_right = jnp.where(swapped, pltpu.roll(from_right, BLOCK, 1), from_right)
    from_left = jnp.where(swapped, pltpu.roll(from_left, BLOCK, 1), from_left)
    second = mm(x_ref[:, 0:WIDTH], v_ref[0])
    third = mm(x_ref[:, WIDTH : 2 * WIDTH], v_ref[1])
    up = jnp.where(first, turned[0], from_left)
    next_up = jnp.where(first, pltpu.roll(turned[0], BLOCK, 1), turned[0])
    down = jnp.where(last, pltpu.roll(turned[1], BLOCK, 1), from_right)
    out_ref[:, 0:WIDTH] = jnp.where(low, up, second)
    out_ref[:, WIDTH : 2 * WIDTH] = jnp.where(low, next_up, third)
    out_ref[:, 2 * WIDTH : 3 * WIDTH] = jnp.where(low, second, turned[1])
    out_ref[:, 3 * WIDTH : 4 * WIDTH] = jnp.where(low, third, down)
    ratio_ref[...] = ratio_in[0:1, 0:1]


def place(turns, inner, turned, landed, ratio):
    rows, wide = inner.shape
    tile = rows // PLACE_STEPS
    return pl.pallas_call(
        functools.partial(place_kernel, lax.axis_size("pair") - 1),
        out_shape=(
            jax.ShapeDtypeStruct((rows, 2 * wide), jnp.float32),
            jax.ShapeDtypeStruct((1, 1), jnp.float32),
        ),
        grid=(PLACE_STEPS,),
        in_specs=[
            pl.BlockSpec(turns.shape, lambda g: (0, 0, 0)),
            pl.BlockSpec((tile, wide), lambda g: (g, 0)),
            pl.BlockSpec((2, tile, WIDTH), lambda g: (0, g, 0)),
            pl.BlockSpec((2, tile, WIDTH), lambda g: (0, lax.rem(g, PLACE_STEPS // 2), 0)),
            pl.BlockSpec((8, WIDTH), lambda g: (0, 0)),
        ],
        out_specs=(
            pl.BlockSpec((tile, 2 * wide), lambda g: (g, 0)),
            pl.BlockSpec((1, 1), lambda g: (0, 0)),
        ),
    )(turns, inner, turned, landed, ratio)


def on_device(r_factor, block_slots):
    turned, landed, inner, grams, ratio = spread(r_factor, block_slots)
    rotated, ratio = place(rotations(grams), inner, turned, landed, ratio)
    return (rotated, ratio.reshape(()))


def solution(mesh):
    in_specs = (P(("row", "pair"), None), P())
    out_specs = (P("row", "pair"), P())
    return jax.shard_map(
        on_device, mesh=mesh, in_specs=in_specs, out_specs=out_specs, check_vma=False
    )
```

```python
import functools

import jax
import jax.numpy as jnp
from jax import lax
from jax.experimental import pallas as pl
from jax.experimental.pallas import tpu as pltpu
from jax.sharding import PartitionSpec as P

BLOCK = 64
ITERS = 3
WIDTH = 2 * BLOCK
MESH = pl.DeviceIdType.MESH
HIGHEST = lax.Precision.HIGHEST
SERIES_TOL = 3e-8
X_CHIPS = 4
EARLY = 8
FACTORS = 8
AT_LEAST = 3
BEFORE = 2
PLACE_STEPS = 2


def mm(lhs, rhs, lhs_dim=1):
    return lax.dot_general(
        lhs,
        rhs,
        (((lhs_dim,), (0,)), ((), ())),
        precision=HIGHEST,
        preferred_element_type=jnp.float32,
    )


def lanes(shape):
    return lax.broadcasted_iota(jnp.int32, shape, len(shape) - 1)


def unit_mask():
    return lax.broadcasted_iota(jnp.int32, (WIDTH, WIDTH), 0) == lanes((WIDTH, WIDTH))


def skew_of(gram, unit):
    on_diag = jnp.where(unit, gram, 0.0)
    d_col = jnp.sum(on_diag, axis=1, keepdims=True)
    d_row = jnp.sum(on_diag, axis=0, keepdims=True)
    return gram * (d_col - d_row) / (2.0 * (d_col * d_col + d_row * d_row))


def series_start(state, skew, square, bound, unit):
    eye = jnp.where(unit, 1.0, 0.0).astype(jnp.float32)
    scale = 2.0 / (2.0 + bound)
    state[0:WIDTH, :] = scale * (eye - 2.0 * skew + square)
    state[WIDTH:, :] = eye - scale * (eye - square)


def series_step(state, reach, unit):
    square = reach * reach
    scale = 2.0 / (2.0 - square)
    both = mm(state[...], state[WIDTH:, :])
    state[0:WIDTH, :] = scale * (state[0:WIDTH, :] + both[0:WIDTH])
    state[WIDTH:, :] = scale * both[WIDTH:] + jnp.where(unit, 1.0 - scale, 0.0)
    return square / (2.0 - square)


def sweep_end(sweep, tall, state):
    v = state[0:WIDTH, :]
    if sweep == 0:
        tall[0:WIDTH, :] = mm(v, mm(tall[0:WIDTH, :], v), 0)
        tall[WIDTH:, :] = v
    elif sweep + 1 < ITERS:
        both = mm(tall[...], v)
        tall[0:WIDTH, :] = mm(v, both[0:WIDTH], 0)
        tall[WIDTH:, :] = both[WIDTH:]
    else:
        tall[WIDTH:, :] = mm(tall[WIDTH:, :], v)


def spread_kernel(
    xs, ys, zs, slots_ref, r_hbm, turned_hbm, landed, x_hbm, g_ref, ratio_ref,
    r_ref, blocks, stage, held, part, half_in, mine, z_in, full,
    tall, state, v_pair, turned, packed, sum_x, sum_y,
    out_send, out_recv, half_send, half_recv, rs_send, rs_recv, ag_send, ag_recv,
    load_sem, save_sem, v_send, v_recv, edge_send, edge_recv, g_send, g_recv,
    x_send, x_recv, y_send, y_recv,
):
    count = xs * ys
    load = pltpu.make_async_copy(r_hbm, r_ref, load_sem)
    load.start()
    me = lax.axis_index("pair")
    row = lax.axis_index("row")
    z, core = row // 2, row % 2
    other = z * 2 + (1 - core)
    rows = r_ref.shape[0]
    steps = held.shape[0]
    half = mine.shape[1]
    chunk = half // zs
    low = lanes((rows, WIDTH)) < BLOCK

    def target(k):
        return lax.rem(me + k, count)

    def z_row(k):
        return lax.rem(z + k, zs) * 2 + core

    barrier = pltpu.get_barrier_semaphore()
    y, x = me // xs, me % xs

    def x_peer(k):
        return y * xs + lax.rem(x + k, xs)

    def y_peer(k):
        return lax.rem(y + k, ys) * xs + x

    for k in range(xs):
        pl.semaphore_signal(
            barrier, inc=1, device_id={"pair": x_peer(k), "row": other}, device_id_type=MESH
        )
    for k in range(1, zs):
        pl.semaphore_signal(barrier, inc=1, device_id={"row": z_row(k)}, device_id_type=MESH)

    def greet(k, carry):
        pl.semaphore_signal(barrier, inc=1, device_id={"pair": target(k)}, device_id_type=MESH)
        return carry

    lax.fori_loop(1, count, greet, 0)

    def lift(t, carry):
        tile = r_ref[:, pl.ds(pl.multiple_of(t * WIDTH, WIDTH), WIDTH)]
        blocks[2 * t] = tile
        blocks[2 * t + 1] = pltpu.roll(tile, BLOCK, 1)
        return carry

    load.wait()
    lax.fori_loop(0, blocks.shape[0] // 2, lift, 0, unroll=8)

    def piece(group, s, i):
        slot = group * 8 + 2 * (1 + i if s else 3 * i)
        upper = blocks[slots_ref[slot]]
        lower = blocks[slots_ref[slot + 1]]
        return jnp.where(low, upper, pltpu.roll(lower, BLOCK, 1))

    def arrange(s):
        def body(k, carry):
            group = target(k)
            for i in range(2):
                stage[s, group, :, i * WIDTH : (i + 1) * WIDTH] = piece(group, s, i)
            return carry

        return body

    here = pl.ds(pl.multiple_of(me * rows, rows), rows)

    def send(s, k):
        return pltpu.make_async_remote_copy(
            src_ref=stage.at[s, target(k)],
            dst_ref=held.at[s, here],
            send_sem=out_send.at[s, k],
            recv_sem=out_recv.at[s, count - k],
            device_id={"pair": target(k)},
            device_id_type=MESH,
        )

    def start(s):
        def body(k, carry):
            send(s, k).start()
            return carry

        return body

    def both(s):
        def body(k, carry):
            arrange(s)(k, carry)
            send(s, k).start()
            return carry

        return body

    def finish(s):
        def body(k, carry):
            send(s, k).wait_recv()
            if s == 1:
                send(s, k).wait_send()
            return carry

        return body

    lax.fori_loop(1, EARLY, arrange(0), 0)
    pl.semaphore_wait(barrier, xs + zs - 1 + count - 1)
    lax.fori_loop(1, EARLY, start(0), 0)
    lax.fori_loop(EARLY, count, both(0), 0)
    for s in range(steps):
        for i in range(2):
            held[s, here, i * WIDTH : (i + 1) * WIDTH] = piece(me, s, i)

    def follow(k, carry):
        arrange(1)(k, carry)
        send(0, k).wait_send()
        send(1, k).start()
        return carry

    lax.fori_loop(1, count, follow, 0)

    def gram(s, i):
        cols = held[s, :, pl.ds(pl.multiple_of(i * WIDTH, WIDTH), WIDTH)]
        part[s, pl.ds(pl.multiple_of(i * WIDTH, WIDTH), WIDTH), :] = mm(cols, cols, 0)

    def save_turned(side):
        return pltpu.make_async_copy(turned.at[side], turned_hbm.at[side], save_sem.at[side])

    def edge_copy(side):
        return pltpu.make_async_remote_copy(
            src_ref=packed.at[side],
            dst_ref=landed.at[side],
            send_sem=edge_send.at[side],
            recv_sem=edge_recv.at[side],
            device_id={"pair": lax.rem(me + count + 2 * side - 1, count)},
            device_id_type=MESH,
        )

    unit = unit_mask()

    def edge_sweep(sweep):
        if sweep == 0:
            tall[0:WIDTH, :] = full[0]
        skew = skew_of(tall[0:WIDTH, :], unit)
        cells = jnp.sum(skew * skew, axis=0, keepdims=True)
        bound = 0.5 * jnp.sum(cells, axis=1, keepdims=True)
        series_start(state, skew, mm(skew, skew), bound, unit)

        def factor(k, reach):
            return series_step(state, reach, unit)

        lax.fori_loop(0, FACTORS, factor, bound / (2.0 + bound), unroll=4)
        sweep_end(sweep, tall, state)

    v_swap = pltpu.make_async_remote_copy(
        src_ref=v_pair.at[core],
        dst_ref=v_pair.at[core],
        send_sem=v_send,
        recv_sem=v_recv,
        device_id={"row": other},
        device_id_type=MESH,
    )

    def send_edges():
        edge_rows = turned.shape[1] // 2
        lane = lanes((edge_rows, WIDTH))
        for side in range(2):
            turned[side] = mm(held[0, :, side * WIDTH : (side + 1) * WIDTH], v_pair[side])
            save_turned(side).start()
            keep = (lane < BLOCK) == (side == 1)
            value = turned.at[side]
            rolled = pltpu.roll(value[edge_rows:, :], BLOCK, 1)
            packed[side] = jnp.where(keep, value[0:edge_rows, :], rolled)
            edge_copy(side).start()

    own = pl.ds(pl.multiple_of(z * chunk, chunk), chunk)
    for s in range(steps):
        lax.fori_loop(1, count, finish(s), 0)
        if s == 1:
            save = pltpu.make_async_copy(held.at[s], x_hbm, save_sem.at[2])
            save.start()
        gram(s, 1 - core)
        swap = pltpu.make_async_remote_copy(
            src_ref=part.at[s, pl.ds(pl.multiple_of((1 - core) * half, half), half)],
            dst_ref=half_in.at[s],
            send_sem=half_send.at[s],
            recv_sem=half_recv.at[s],
            device_id={"row": other},
            device_id_type=MESH,
        )
        swap.start()
        gram(s, core)
        swap.wait()
        mine[s] = part[s, pl.ds(pl.multiple_of(core * half, half), half), :] + half_in[s]

        def scatter(k, s=s):
            at = pl.multiple_of(lax.rem(z + k, zs) * chunk, chunk)
            return pltpu.make_async_remote_copy(
                src_ref=mine.at[s, pl.ds(at, chunk)],
                dst_ref=z_in.at[s, zs - k],
                send_sem=rs_send.at[s, k],
                recv_sem=rs_recv.at[s, zs - k],
                device_id={"row": z_row(k)},
                device_id_type=MESH,
            )

        for k in range(1, zs):
            scatter(k).start()
        if s == 1:
            for sweep in range(BEFORE, ITERS):
                edge_sweep(sweep)
            v_pair[core] = tall[WIDTH:, :]
        for k in range(1, zs):
            scatter(k).wait()
        total = mine[s, own, :]
        for k in range(1, zs):
            total = total + z_in[s, k]
        full[s, own, :] = total

        def gather(k, s=s):
            return pltpu.make_async_remote_copy(
                src_ref=full.at[s, own],
                dst_ref=full.at[s, own],
                send_sem=ag_send.at[s, k],
                recv_sem=ag_recv.at[s, zs - k],
                device_id={"row": z_row(k)},
                device_id_type=MESH,
            )

        for k in range(1, zs):
            gather(k).start()
        if s == 1:
            v_swap.start()
            v_swap.wait()
            send_edges()
        for k in range(1, zs):
            gather(k).wait()
        if s == 0:
            for sweep in range(BEFORE):
                edge_sweep(sweep)

    pair_g = part.at[0]
    own_g = pl.ds(pl.multiple_of(core * half, half), half)
    pair_g[own_g, :] = full[1]
    g_swap = pltpu.make_async_remote_copy(
        src_ref=full.at[1],
        dst_ref=pair_g.at[own_g],
        send_sem=g_send,
        recv_sem=g_recv,
        device_id={"row": other},
        device_id_type=MESH,
    )

    off = jnp.zeros((1, WIDTH), jnp.float32)
    on = jnp.zeros((1, WIDTH), jnp.float32)
    for s in range(steps):
        squares = full[s] * full[s]
        off = off + jnp.sum(jnp.where(unit, 0.0, squares), axis=0, keepdims=True)
        on = on + jnp.sum(jnp.where(unit, squares, 0.0), axis=0, keepdims=True)
    tile_row = lax.broadcasted_iota(jnp.int32, (8, WIDTH), 0)
    sum_x[core, x] = jnp.where(tile_row == 0, off, jnp.where(tile_row == 1, on, 0.0))

    def x_copy(k, crossed):
        return pltpu.make_async_remote_copy(
            src_ref=sum_x.at[core, x],
            dst_ref=sum_x.at[core, x],
            send_sem=x_send.at[crossed, k],
            recv_sem=x_recv.at[crossed, (xs - k) % xs],
            device_id={"pair": x_peer(k), "row": other if crossed else row},
            device_id_type=MESH,
        )

    x_copies = [x_copy(k, crossed) for crossed in range(2) for k in range(1 - crossed, xs)]
    for copy in x_copies:
        copy.start()
    g_swap.start()
    for copy in x_copies:
        copy.wait()
    total = jnp.zeros((8, WIDTH), jnp.float32)
    for k in range(xs):
        total = total + (sum_x[0, k] + sum_x[1, k])
    sum_y[y] = total

    def y_copy(k):
        return pltpu.make_async_remote_copy(
            src_ref=sum_y.at[y],
            dst_ref=sum_y.at[y],
            send_sem=y_send.at[k],
            recv_sem=y_recv.at[ys - k],
            device_id={"pair": y_peer(k)},
            device_id_type=MESH,
        )

    for k in range(1, ys):
        y_copy(k).start()
    g_swap.wait()
    g_ref[...] = pair_g[...]
    for side in range(2):
        save_turned(side).wait()
        edge_copy(side).wait()
    save.wait()
    for k in range(1, ys):
        y_copy(k).wait()
    total = sum_y[0]
    for k in range(1, ys):
        total = total + sum_y[k]
    off = jnp.sum(total[0:1, :], axis=1, keepdims=True)
    on = jnp.sum(total[1:2, :], axis=1, keepdims=True)
    ratio_ref[...] = jnp.broadcast_to(jnp.sqrt(off / on), ratio_ref.shape)


def spread(r_factor, block_slots):
    rows, cols = r_factor.shape
    count = lax.axis_size("pair")
    xs = X_CHIPS
    ys = count // xs
    zs = lax.axis_size("row") // 2
    steps = 2
    wide = cols // count // steps
    tall_rows = rows * count
    half = WIDTH
    vmem = pl.BlockSpec(memory_space=pltpu.VMEM)
    hbm = pl.BlockSpec(memory_space=pl.ANY)
    dma = pltpu.SemaphoreType.DMA

    def f32(*shape):
        return jax.ShapeDtypeStruct(shape, jnp.float32)

    def work(*shape):
        return pltpu.VMEM(shape, jnp.float32)

    return pl.pallas_call(
        functools.partial(spread_kernel, xs, ys, zs),
        out_shape=(
            f32(2, tall_rows, WIDTH),
            f32(2, tall_rows // 2, WIDTH),
            f32(tall_rows, wide),
            f32(2 * half, WIDTH),
            f32(8, WIDTH),
        ),
        in_specs=[pl.BlockSpec(memory_space=pltpu.SMEM), hbm],
        out_specs=(hbm, hbm, hbm, vmem, vmem),
        scratch_shapes=[
            work(rows, cols),
            work(cols // BLOCK, rows, WIDTH),
            work(steps, count, rows, wide),
            work(steps, tall_rows, wide),
            work(steps, 2 * half, WIDTH),
            work(steps, half, WIDTH),
            work(steps, half, WIDTH),
            work(steps, zs, half // zs, WIDTH),
            work(steps, half, WIDTH),
            work(2 * WIDTH, WIDTH),
            work(2 * WIDTH, WIDTH),
            work(2, WIDTH, WIDTH),
            work(2, tall_rows, WIDTH),
            work(2, tall_rows // 2, WIDTH),
            work(2, xs, 8, WIDTH),
            work(ys, 8, WIDTH),
            dma((steps, count)),
            dma((steps, count)),
            dma((steps,)),
            dma((steps,)),
            dma((steps, zs)),
            dma((steps, zs)),
            dma((steps, zs)),
            dma((steps, zs)),
            dma,
            dma((3,)),
            dma,
            dma,
            dma((2,)),
            dma((2,)),
            dma,
            dma,
            dma((2, xs)),
            dma((2, xs)),
            dma((ys,)),
            dma((ys,)),
        ],
        compiler_params=pltpu.CompilerParams(collective_id=0, has_side_effects=True),
    )(block_slots, r_factor)


def rotation_kernel(g_ref, out_ref, tall, state):
    pairs = tall.shape[0]
    unit = unit_mask()
    for p in range(pairs):
        tall[p, 0:WIDTH, :] = g_ref[p * WIDTH : (p + 1) * WIDTH, :]
    for sweep in range(ITERS):
        most = jnp.zeros((), jnp.float32)
        work = []
        for p in range(pairs):
            skew = skew_of(tall[p, 0:WIDTH, :], unit)
            square = mm(skew, skew)
            bound = jnp.max(jnp.sum(jnp.abs(square), axis=0, keepdims=True))
            work.append((skew, square))
            most = jnp.maximum(most, bound)
        for p in range(pairs):
            series_start(state.at[p], *work[p], most, unit)

        def step(reach):
            for p in range(pairs):
                after = series_step(state.at[p], reach, unit)
            return after

        reach = most / (2.0 + most)
        for _ in range(AT_LEAST):
            reach = step(reach)
        lax.while_loop(lambda left: left > SERIES_TOL, step, reach)
        for p in range(pairs):
            sweep_end(sweep, tall.at[p], state.at[p])
    for p in range(pairs):
        out_ref[p] = tall[p, WIDTH:, :]


def rotations(grams):
    vmem = pl.BlockSpec(memory_space=pltpu.VMEM)
    pairs = grams.shape[0] // WIDTH
    work = pltpu.VMEM((pairs, 2 * WIDTH, WIDTH), jnp.float32)
    return pl.pallas_call(
        rotation_kernel,
        out_shape=jax.ShapeDtypeStruct((pairs, WIDTH, WIDTH), jnp.float32),
        in_specs=[vmem],
        out_specs=vmem,
        scratch_shapes=[work] * 2,
    )(grams)


def place_kernel(last_pair, v_ref, x_ref, turned, landed, ratio_in, out_ref, ratio_ref):
    pair = lax.axis_index("pair")
    first, last = pair == 0, pair == last_pair
    swapped = pl.program_id(0) >= pl.num_programs(0) // 2
    low = lanes(landed.shape[1:]) < BLOCK
    from_right, from_left = landed[0], landed[1]
    from_right = jnp.where(swapped, pltpu.roll(from_right, BLOCK, 1), from_right)
    from_left = jnp.where(swapped, pltpu.roll(from_left, BLOCK, 1), from_left)
    second = mm(x_ref[:, 0:WIDTH], v_ref[0])
    third = mm(x_ref[:, WIDTH : 2 * WIDTH], v_ref[1])
    up = jnp.where(first, turned[0], from_left)
    next_up = jnp.where(first, pltpu.roll(turned[0], BLOCK, 1), turned[0])
    down = jnp.where(last, pltpu.roll(turned[1], BLOCK, 1), from_right)
    out_ref[:, 0:WIDTH] = jnp.where(low, up, second)
    out_ref[:, WIDTH : 2 * WIDTH] = jnp.where(low, next_up, third)
    out_ref[:, 2 * WIDTH : 3 * WIDTH] = jnp.where(low, second, turned[1])
    out_ref[:, 3 * WIDTH : 4 * WIDTH] = jnp.where(low, third, down)
    ratio_ref[...] = ratio_in[0:1, 0:1]


def place(turns, inner, turned, landed, ratio):
    rows, wide = inner.shape
    tile = rows // PLACE_STEPS
    return pl.pallas_call(
        functools.partial(place_kernel, lax.axis_size("pair") - 1),
        out_shape=(
            jax.ShapeDtypeStruct((rows, 2 * wide), jnp.float32),
            jax.ShapeDtypeStruct((1, 1), jnp.float32),
        ),
        grid=(PLACE_STEPS,),
        in_specs=[
            pl.BlockSpec(turns.shape, lambda g: (0, 0, 0)),
            pl.BlockSpec((tile, wide), lambda g: (g, 0)),
            pl.BlockSpec((2, tile, WIDTH), lambda g: (0, g, 0)),
            pl.BlockSpec((2, tile, WIDTH), lambda g: (0, lax.rem(g, PLACE_STEPS // 2), 0)),
            pl.BlockSpec((8, WIDTH), lambda g: (0, 0)),
        ],
        out_specs=(
            pl.BlockSpec((tile, 2 * wide), lambda g: (g, 0)),
            pl.BlockSpec((1, 1), lambda g: (0, 0)),
        ),
    )(turns, inner, turned, landed, ratio)


def on_device(r_factor, block_slots):
    turned, landed, inner, grams, ratio = spread(r_factor, block_slots)
    rotated, ratio = place(rotations(grams), inner, turned, landed, ratio)
    return (rotated, ratio.reshape(()))


def solution(mesh):
    in_specs = (P(("row", "pair"), None), P())
    out_specs = (P("row", "pair"), P())
    return jax.shard_map(
        on_device, mesh=mesh, in_specs=in_specs, out_specs=out_specs, check_vma=False
    )
```
